128 devices in a mesh: smp: 8 (over y, core), gx: 8 (over z_lo, x), gz: 2 (over z_hi).
Axes of the slice: x: 4, y: 4, z: 4 (z_hi: 2, z_lo: 2; z = z_hi * 2 + z_lo), core: 2. Of those that a mesh axis runs over, the one named last changes fastest.
Arguments:
- features: bfloat16 [8, 32, 40, 8, 256], P('smp', None, 'gx', None, 'gz'), may hold values from -6 to 6
- first_weight: bfloat16 [32, 3, 3, 3, 32], replicated, may hold values from -0.21875 to 0.21875
- first_bias: float32 [32], replicated, may hold values from -1 to 1
- second_weight: bfloat16 [32, 3, 3, 3, 32], replicated, may hold values from -0.21875 to 0.21875
- second_bias: float32 [32], replicated, may hold values from -1 to 1
- cotangent: bfloat16 [8, 32, 40, 8, 256], P('smp', None, 'gx', None, 'gz'), may hold values from -6 to 6
Outputs:
- output: bfloat16 [8, 32, 40, 8, 256], P('smp', None, 'gx', None, 'gz')
- first_grad: float32 [32, 3, 3, 3, 32], replicated
- first_bias_grad: float32 [32], replicated
- second_grad: float32 [32, 3, 3, 3, 32], replicated
- second_bias_grad: float32 [32], replicated
The draws below stay inside these ranges and needn't reach their ends.
All inputs are finite; a program needn't handle non-finite values.
Results may differ from the reference program's by a relative error of at most 0.011.
Values may be sent and summed in bfloat16 or wider, within the bound.
A program may use at most 128 MiB of HBM per device.

```python
import math
import jax
import jax.numpy as jnp
from jax import lax

C = 32
NY = 8
SAMPLES = 8
NX = 40
NZ = 256
CELLS = 655360


def levels(key, extent, pieces, least, largest):
    def one(position, blocks):
        heights = jax.random.uniform(jax.random.fold_in(jax.random.fold_in(key, 6), position), (blocks,), jnp.float32, least / len(pieces), largest / len(pieces))
        return jnp.repeat(jnp.exp(heights), extent[position] // blocks).reshape((-1,) + (1,) * (len(extent) - position - 1))

    loudness = one(*pieces[0])
    for cut in pieces[1:]:
        loudness = loudness * one(*cut)
    return loudness


def bell_draw(own_key, dims, scale, most, cuts=(), held_as=jnp.bfloat16):
    drawn = jax.random.normal(own_key, dims, jnp.float32) * scale
    if len(cuts) > 0:
        drawn = levels(own_key, dims, cuts, -0.22, 0.18) * drawn
    return jnp.clip(drawn, min=-most, max=most).astype(held_as)


def setup_inputs(seed: int = 0) -> dict:
    seeds = jax.random.split(jax.random.key(seed), 7)
    features = bell_draw(seeds[0], (SAMPLES, C, NX, NY, NZ), 1.0, 6.0, ((0, 8), (2, 8), (4, 2)))
    first_weight = bell_draw(seeds[1], (C, 3, 3, 3, C), (27 * C) ** -0.5, 0.21875)
    first_bias = jnp.clip(jax.random.uniform(seeds[2], (C,), jnp.float32, -1.0, 1.0), -1.0, 1.0)
    second_weight = bell_draw(seeds[3], (C, 3, 3, 3, C), (27 * C) ** -0.5, 0.21875)
    second_bias = jnp.clip(jax.random.uniform(seeds[4], (C,), jnp.float32, -1.0, 1.0), -1.0, 1.0)
    cotangent = bell_draw(seeds[5], (SAMPLES, C, NX, NY, NZ), 1.0, 6.0, ((0, 8), (2, 8), (4, 2)))
    return {"features": features, "first_weight": first_weight, "first_bias": first_bias, "second_weight": second_weight, "second_bias": second_bias, "cotangent": cotangent}


def pad_field(field_in):
    wrapped = jnp.pad(field_in, ((0, 0), (0, 0), (1, 1), (0, 0), (1, 1)), mode='wrap')
    return jnp.pad(wrapped, ((0, 0), (0, 0), (0, 0), (1, 1), (0, 0))).astype(jnp.float32)

def window(padded, offset_x, offset_y, offset_z, shape):
    return padded[:, :, offset_x:offset_x + shape[2], offset_y:offset_y + shape[3], offset_z:offset_z + shape[4]]

def convolve(padded, weight, shape):
    weight_f = weight.astype(jnp.float32)
    summed = jnp.zeros((shape[0], weight.shape[0], shape[2], shape[3], shape[4]), jnp.float32)
    for offset_x in range(3):
        for offset_y in range(3):
            for offset_z in range(3):
                summed = summed + jnp.einsum('oi,sixyz->soxyz', weight_f[:, offset_x, offset_y, offset_z], window(padded, offset_x, offset_y, offset_z, shape), precision=lax.Precision.HIGHEST)
    return summed

def correlate(upstream, padded):
    shape = upstream.shape
    upstream_f = upstream.astype(jnp.float32)
    tap_terms = []
    for offset_x in range(3):
        for offset_y in range(3):
            for offset_z in range(3):
                tap_terms.append(jnp.einsum('soxyz,sixyz->oi', upstream_f, window(padded, offset_x, offset_y, offset_z, shape), precision=lax.Precision.HIGHEST))
    stacked = jnp.stack(tap_terms, axis=1)
    return stacked.reshape(shape[1], 3, 3, 3, padded.shape[1])

def reference(features, first_weight, first_bias, second_weight, second_bias, cotangent):
    grad_scale = 1.0 / math.sqrt(CELLS)
    flipped = jnp.transpose(jnp.flip(second_weight, (1, 2, 3)), (4, 1, 2, 3, 0))
    outputs = []
    first_grad = jnp.zeros(first_weight.shape, jnp.float32)
    second_grad = jnp.zeros(second_weight.shape, jnp.float32)
    first_bgrad = jnp.zeros(first_bias.shape, jnp.float32)
    second_bgrad = jnp.zeros(second_bias.shape, jnp.float32)
    for sample in range(SAMPLES):
        field_in = features[sample:sample + 1]
        shape = field_in.shape
        input_pad = pad_field(field_in)
        preact = convolve(input_pad, first_weight, shape) + first_bias[None, :, None, None, None]
        hidden = jax.nn.silu(preact).astype(jnp.bfloat16)
        hidden_pad = pad_field(hidden)
        residual_term = convolve(hidden_pad, second_weight, shape) + second_bias[None, :, None, None, None]
        outputs.append((field_in.astype(jnp.float32) + residual_term).astype(jnp.bfloat16))
        upstream = cotangent[sample:sample + 1]
        second_grad = second_grad + correlate(upstream, hidden_pad)
        second_bgrad = second_bgrad + lax.optimization_barrier(jnp.sum(upstream.astype(jnp.float32), axis=(0, 2, 3, 4)))
        hidden_grad = convolve(pad_field(upstream), flipped, shape)
        logistic = jax.nn.sigmoid(preact)
        preact_grad = (hidden_grad * logistic * (1.0 + preact * (1.0 - logistic))).astype(jnp.bfloat16)
        first_grad = first_grad + correlate(preact_grad, input_pad)
        first_bgrad = first_bgrad + lax.optimization_barrier(jnp.sum(preact_grad.astype(jnp.float32), axis=(0, 2, 3, 4)))
    return (jnp.concatenate(outputs, 0), first_grad * grad_scale, first_bgrad * grad_scale, second_grad * grad_scale, second_bgrad * grad_scale)
```

```python
import functools

import jax
import jax.numpy as jnp
from jax import lax
from jax.experimental import pallas as pl
from jax.experimental.pallas import tpu as pltpu
from jax.sharding import PartitionSpec as P

MESH = pl.DeviceIdType.MESH
BF = jnp.bfloat16
F32 = jnp.float32
LANES = 128
PAY = 640


def kernel(sizes, scale, ft, ct, w1, w2, w2t, b1, b2, out, g1, gb1, g2, gb2,
           sf, sc, sh, eo, ei, wa, wb, wv, dd, pg, pay, snd, ra, mid, rb, fin, rc,
           hs, hr, as_, ar, bs, br, cs, cr):
    ns, nx, nz = sizes
    ng = nx * nz
    rows = PAY // ng
    smp, gx, gz = lax.axis_index("smp"), lax.axis_index("gx"), lax.axis_index("gz")
    me = gx * nz + gz
    left, right = lax.rem(gx + nx - 1, nx), lax.rem(gx + 1, nx)
    other = 1 - gz
    lane = lax.broadcasted_iota(jnp.int32, (32, LANES), 1)
    half = lane // 2

    def in_group(d):
        peer = lax.rem(me + d, ng)
        return peer, (smp, peer // nz, lax.rem(peer, nz))

    def in_samples(d):
        peer = lax.rem(smp + d, ns)
        return peer, (peer, gx, gz)

    barrier = pltpu.get_barrier_semaphore()

    @pl.loop(1, ng)
    def _(d):
        pl.semaphore_signal(barrier, inc=1, device_id=in_group(d)[1], device_id_type=MESH)

    @pl.loop(1, ns)
    def _(d):
        pl.semaphore_signal(barrier, inc=1, device_id=in_samples(d)[1], device_id_type=MESH)

    def edges(s, f):
        def body(j, acc):
            row = pl.multiple_of(lax.rem(j, 8) * 32, 32)
            blk = s[1, 1 + j // 8, pl.ds(row, 32), :].astype(F32)
            return jnp.where(half == j, pltpu.roll(blk, 2 * j + 1, 1), acc)

        eo[f] = lax.fori_loop(0, 40, body, jnp.zeros((32, LANES), F32), unroll=8).astype(BF)

    def halo(s, f):
        plan = (
            (2, eo.at[f], ei.at[f, 1], (smp, gx, other)),
            (3, eo.at[f], ei.at[f, 2], (smp, left, other)),
            (4, eo.at[f], ei.at[f, 0], (smp, right, other)),
            (0, s.at[1, 1], s.at[1, 6], (smp, left, gz)),
            (1, s.at[1, 5], s.at[1, 0], (smp, right, gz)),
        )
        return [
            pltpu.make_async_remote_copy(
                src_ref=src, dst_ref=dst, send_sem=hs.at[f, i], recv_sem=hr.at[f, i],
                device_id=dev, device_id_type=MESH,
            )
            for i, src, dst, dev in plan
        ]

    def shift(s, f):
        for slots, which, first in (((1, 6), 1, 0), ((0, 1), 0, 32), ((6, 7), 2, 0)):
            edge = ei[f, which].astype(F32)

            def body(j, carry, edge=edge, first=first, slot0=slots[0]):
                slot = slot0 + j // 8
                row = pl.multiple_of(lax.rem(j, 8) * 32, 32)
                blk = s[1, slot, pl.ds(row, 32), :].astype(F32)
                e = pltpu.roll(edge, 127 - 2 * (first + j), 1)
                s[0, slot, pl.ds(row, 32), :] = pltpu.roll(jnp.where(lane == 127, e, blk), 1, 1).astype(BF)
                s[2, slot, pl.ds(row, 32), :] = pltpu.roll(jnp.where(lane == 0, e, blk), 127, 1).astype(BF)
                return carry

            lax.fori_loop(0, 8 * (slots[1] - slots[0]), body, 0, unroll=8)

    def banded(dst, tap):
        zero = jnp.zeros((32, LANES), F32)
        for k in range(9):
            a, c = k // 3, k % 3
            parts = [tap(a * 9 + b * 3 + c).astype(F32) for b in range(3)]
            base = jnp.concatenate(parts + [jnp.zeros((32, 32), F32)], axis=1)
            r = [pltpu.roll(base, (32 * (m + 3)) % LANES, 1) if m != 1 else base for m in range(4)]
            low, mid_, top = lane < 32, lane < 64, lane >= 96
            tiles = (
                (jnp.where(mid_, r[0], 0.0), zero),
                (r[1], zero),
                (r[2], zero),
                (jnp.where(mid_, 0.0, r[3]), jnp.where(low, r[3], 0.0)),
                (jnp.where(top, r[0], 0.0), jnp.where(mid_, r[0], 0.0)),
                (zero, r[1]),
                (zero, r[2]),
                (zero, jnp.where(mid_, 0.0, r[3])),
            )
            for y, pair in enumerate(tiles):
                for t in range(2):
                    dst[k, y * 32:(y + 1) * 32, t * LANES:(t + 1) * LANES] = pair[t].astype(BF)

    def conv(w, s, xs):
        lhs = jnp.concatenate([w[k] for k in range(9)], axis=1)
        rhs = jnp.concatenate(
            [jnp.concatenate([s[k % 3, x + k // 3] for x in xs], axis=1) for k in range(9)], axis=0)
        return jnp.dot(lhs, rhs, preferred_element_type=F32)

    def diagonal(g):
        t = [[g[y * 32:(y + 1) * 32, u * LANES:(u + 1) * LANES] for u in range(2)] for y in range(8)]
        x0 = jnp.where(lane < 64, t[0][0] + t[4][1], jnp.where(lane >= 96, t[4][0], 0.0))
        x1 = t[1][0] + t[5][1]
        x2 = t[2][0] + t[6][1]
        x3 = jnp.where(lane >= 64, t[3][0] + t[7][1], jnp.where(lane < 32, t[3][1], 0.0))
        total = pltpu.roll(x0, 32, 1) + x1 + pltpu.roll(x2, 96, 1) + pltpu.roll(x3, 64, 1)
        return jnp.where(lane < 96, total, 0.0)

    def column(ref):
        row = lax.broadcasted_iota(jnp.int32, (32, 32), 0)
        col = lax.broadcasted_iota(jnp.int32, (32, 32), 1)
        one = jnp.sum(jnp.where(row == col, jnp.broadcast_to(ref[...], (32, 32)), 0.0), axis=1, keepdims=True)
        return jnp.concatenate([one] * 8, axis=0)

    for x in range(5):
        sf[1, 1 + x] = ft[x]
        sc[1, 1 + x] = ct[x]
    edges(sf, 0)
    edges(sc, 1)
    pl.semaphore_wait(barrier, ng + ns - 2)
    moves_f = halo(sf, 0)
    for m in moves_f:
        m.start()
    moves_c = halo(sc, 1)
    for m in moves_c:
        m.start()

    banded(wa, lambda i: w1[i])
    banded(wv, lambda i: w2t[26 - i])
    banded(wb, lambda i: w2[i])

    for m in moves_f:
        m.wait_recv()
    shift(sf, 0)
    tiles = ((0, 1), (2, 3), (4,))
    bias = column(b1)
    for xs in tiles:
        v = conv(wa, sf, xs) + bias
        q = 1.0 / (1.0 + jnp.exp(-v))
        h = (v * q).astype(BF)
        d = q * (1.0 + v * (1.0 - q))
        for i, x in enumerate(xs):
            sh[1, 1 + x] = h[:, i * LANES:(i + 1) * LANES]
            dd[x] = d[:, i * LANES:(i + 1) * LANES]
    edges(sh, 2)
    moves_h = halo(sh, 2)
    for m in moves_h:
        m.start()

    for m in moves_c:
        m.wait_recv()
    shift(sc, 1)
    sums = jnp.zeros((256, LANES), F32)
    for xs in tiles:
        u = conv(wv, sc, xs)
        for i, x in enumerate(xs):
            p = (u[:, i * LANES:(i + 1) * LANES] * dd[x]).astype(BF)
            pg[x] = p
            sums = sums + p.astype(F32)

    def spans(s, c, a):
        return jnp.concatenate([s[c, a + x] for x in range(5)], axis=1)

    def nt(p, r):
        return lax.dot_general(p, r, (((1,), (1,)), ((), ())), preferred_element_type=F32)

    for k in range(9):
        a, c = k // 3, k % 3
        upstream = jnp.concatenate([pg[x] for x in range(5)], axis=1)
        pay[k * 32:(k + 1) * 32] = diagonal(nt(upstream, spans(sf, c, a)))
    for k in range(9):
        a, c = k // 3, k % 3
        own = jnp.concatenate([sh[1, 1 + x] for x in range(5)], axis=1)
        pay[288 + k * 32:288 + (k + 1) * 32] = diagonal(nt(spans(sc, 2 - c, 2 - a), own))

    def folded(v):
        total = v[0:32]
        for y in range(1, 8):
            total = total + v[y * 32:(y + 1) * 32]
        return jnp.sum(total, axis=1, keepdims=True)

    csum = jnp.zeros((256, LANES), F32)
    for x in range(5):
        csum = csum + ct[x].astype(F32)
    pay[576:608] = jnp.where(lane == 0, folded(sums), jnp.where(lane == 1, folded(csum), 0.0))
    pay[608:640] = jnp.zeros((32, LANES), F32)

    for s in range(ng):
        snd[s] = pay[s * rows:(s + 1) * rows].astype(BF)

    def send_a(d):
        peer, dev = in_group(d)
        return pltpu.make_async_remote_copy(
            src_ref=snd.at[peer], dst_ref=ra.at[me], send_sem=as_.at[peer], recv_sem=ar.at[me],
            device_id=dev, device_id_type=MESH)

    def from_a(d):
        peer, dev = in_group(d)
        return pltpu.make_async_remote_copy(
            src_ref=snd.at[peer], dst_ref=ra.at[peer], send_sem=as_.at[peer], recv_sem=ar.at[peer],
            device_id=dev, device_id_type=MESH)

    @pl.loop(1, ng)
    def _(d):
        send_a(d).start()

    ra[me] = snd[me]

    for m in moves_h:
        m.wait_recv()
    shift(sh, 2)
    bias2 = column(b2)
    for xs in tiles:
        v = conv(wb, sh, xs) + bias2
        for i, x in enumerate(xs):
            out[x] = (v[:, i * LANES:(i + 1) * LANES] + ft[x].astype(F32)).astype(BF)

    @pl.loop(1, ng)
    def _(d):
        from_a(d).wait_recv()

    def total(ref, n):
        acc = ref[0].astype(F32)
        for s in range(1, n):
            acc = acc + ref[s].astype(F32)
        return acc

    mid[...] = total(ra, ng).astype(BF)

    def send_b(d):
        peer, dev = in_samples(d)
        return pltpu.make_async_remote_copy(
            src_ref=mid, dst_ref=rb.at[smp], send_sem=bs.at[peer], recv_sem=br.at[smp],
            device_id=dev, device_id_type=MESH)

    def from_b(d):
        peer, dev = in_samples(d)
        return pltpu.make_async_remote_copy(
            src_ref=mid, dst_ref=rb.at[peer], send_sem=bs.at[peer], recv_sem=br.at[peer],
            device_id=dev, device_id_type=MESH)

    @pl.loop(1, ns)
    def _(d):
        send_b(d).start()

    rb[smp] = mid[...]

    @pl.loop(1, ns)
    def _(d):
        from_b(d).wait_recv()

    fin[...] = (total(rb, ns) * scale).astype(BF)

    def send_c(d):
        peer, dev = in_group(d)
        return pltpu.make_async_remote_copy(
            src_ref=fin, dst_ref=rc.at[me], send_sem=cs.at[peer], recv_sem=cr.at[me],
            device_id=dev, device_id_type=MESH)

    def from_c(d):
        peer, dev = in_group(d)
        return pltpu.make_async_remote_copy(
            src_ref=fin, dst_ref=rc.at[peer], send_sem=cs.at[peer], recv_sem=cr.at[peer],
            device_id=dev, device_id_type=MESH)

    @pl.loop(1, ng)
    def _(d):
        send_c(d).start()

    rc[me] = fin[...]

    @pl.loop(1, ng)
    def _(d):
        from_c(d).wait_recv()

    for s in range(ng):
        pay[s * rows:(s + 1) * rows] = rc[s].astype(F32)
    for base, ref in ((0, g1), (288, g2)):
        for k in range(9):
            a, c = k // 3, k % 3
            blk = pay[base + k * 32:base + (k + 1) * 32]
            for b in range(3):
                ref[a * 9 + b * 3 + c] = blk[:, b * 32:(b + 1) * 32]
    tail = pay[576:608]
    row = lax.broadcasted_iota(jnp.int32, (32, 32), 0)
    col = lax.broadcasted_iota(jnp.int32, (32, 32), 1)
    for i, ref in ((0, gb1), (1, gb2)):
        ref[...] = jnp.sum(jnp.where(row == col, tail[:, i:i + 1], 0.0), axis=0, keepdims=True)

    for m in moves_f + moves_c + moves_h:
        m.wait_send()

    @pl.loop(1, ng)
    def _(d):
        send_a(d).wait_send()

    @pl.loop(1, ns)
    def _(d):
        send_b(d).wait_send()

    @pl.loop(1, ng)
    def _(d):
        send_c(d).wait_send()


def solution(mesh):
    sizes = tuple(mesh.shape[n] for n in ("smp", "gx", "gz"))
    ns, nx, nz = sizes
    ng = nx * nz
    rows = PAY // ng

    def slabs(field):
        return field[0].transpose(1, 2, 0, 3).reshape(5, 256, LANES)

    def shards(features, first_weight, first_bias, second_weight, second_bias, cotangent):
        cells = ns * nx * nz * 5 * 8 * LANES
        w1 = first_weight.transpose(1, 2, 3, 0, 4).reshape(27, 32, 32)
        w2 = second_weight.transpose(1, 2, 3, 0, 4).reshape(27, 32, 32)
        w2t = second_weight.transpose(1, 2, 3, 4, 0).reshape(27, 32, 32)
        vm = pl.BlockSpec(memory_space=pltpu.VMEM)
        dma = pltpu.SemaphoreType.DMA
        out, g1, gb1, g2, gb2 = pl.pallas_call(
            functools.partial(kernel, sizes, cells ** -0.5),
            out_shape=(
                jax.ShapeDtypeStruct((5, 256, LANES), BF),
                jax.ShapeDtypeStruct((27, 32, 32), F32),
                jax.ShapeDtypeStruct((1, 32), F32),
                jax.ShapeDtypeStruct((27, 32, 32), F32),
                jax.ShapeDtypeStruct((1, 32), F32),
            ),
            in_specs=[vm] * 7,
            out_specs=(vm,) * 5,
            scratch_shapes=[
                pltpu.VMEM((3, 7, 256, LANES), BF),
                pltpu.VMEM((3, 7, 256, LANES), BF),
                pltpu.VMEM((3, 7, 256, LANES), BF),
                pltpu.VMEM((3, 32, LANES), BF),
                pltpu.VMEM((3, 3, 32, LANES), BF),
                pltpu.VMEM((9, 256, 256), BF),
                pltpu.VMEM((9, 256, 256), BF),
                pltpu.VMEM((9, 256, 256), BF),
                pltpu.VMEM((5, 256, LANES), F32),
                pltpu.VMEM((5, 256, LANES), BF),
                pltpu.VMEM((PAY, LANES), F32),
                pltpu.VMEM((ng, rows, LANES), BF),
                pltpu.VMEM((ng, rows, LANES), BF),
                pltpu.VMEM((rows, LANES), BF),
                pltpu.VMEM((ns, rows, LANES), BF),
                pltpu.VMEM((rows, LANES), BF),
                pltpu.VMEM((ng, rows, LANES), BF),
                dma((3, 5)), dma((3, 5)),
                dma((ng,)), dma((ng,)), dma((ns,)), dma((ns,)), dma((ng,)), dma((ng,)),
            ],
            compiler_params=pltpu.CompilerParams(
                collective_id=0, has_side_effects=True, vmem_limit_bytes=48 << 20),
        )(slabs(features), slabs(cotangent), w1, w2, w2t, first_bias.reshape(1, 32), second_bias.reshape(1, 32))
        back = lambda g: g.reshape(3, 3, 3, 32, 32).transpose(3, 0, 1, 2, 4)
        output = out.reshape(5, 8, 32, LANES).transpose(2, 0, 1, 3)[None]
        return output, back(g1), gb1.reshape(32), back(g2), gb2.reshape(32)

    block = P("smp", None, "gx", None, "gz")
    return jax.shard_map(
        shards, mesh=mesh, in_specs=(block, P(), P(), P(), P(), block),
        out_specs=(block, P(), P(), P(), P()), check_vma=False)
```

```python
import functools

import jax
import jax.numpy as jnp
from jax import lax
from jax.experimental import pallas as pl
from jax.experimental.pallas import tpu as pltpu
from jax.sharding import PartitionSpec as P

MESH = pl.DeviceIdType.MESH
BF = jnp.bfloat16
F32 = jnp.float32
LANES = 128
PAY = 640


def kernel(sizes, scale, feat, cot, w1h, w2h, b1h, b2h, rc, out,
           vf, vc, w1, w2, b1, b2, pm, pe, ps,
           sf, sc, sh, eo, ei, wa, wb, wv, dd, pg, pay, snd, ra, mid, rb, fin,
           ins, hs, hr, as_, ar, bs, br, cs, cr):
    ns, nx, nz = sizes
    ng = nx * nz
    rows = PAY // ng
    smp, gx, gz = lax.axis_index("smp"), lax.axis_index("gx"), lax.axis_index("gz")
    me = gx * nz + gz
    left, right = lax.rem(gx + nx - 1, nx), lax.rem(gx + 1, nx)
    other = 1 - gz
    lane = lax.broadcasted_iota(jnp.int32, (32, LANES), 1)
    level = lax.rem(lane // 2, 8)

    def in_group(d):
        peer = lax.rem(me + d, ng)
        return peer, (smp, peer // nz, lax.rem(peer, nz))

    def in_samples(d):
        peer = lax.rem(smp + d, ns)
        return peer, (peer, gx, gz)

    load_f = [pltpu.make_async_copy(feat.at[:, x], vf.at[x], ins.at[x]) for x in range(5)]
    load_c = [pltpu.make_async_copy(cot.at[:, x], vc.at[x], ins.at[5 + x]) for x in range(5)]
    load_w = [
        pltpu.make_async_copy(src, dst, ins.at[10 + i])
        for i, (src, dst) in enumerate(((w1h, w1), (w2h, w2), (b1h, b1), (b2h, b2)))
    ]
    for m in load_f + load_c + load_w:
        m.start()

    barrier = pltpu.get_barrier_semaphore()

    @pl.loop(1, ng)
    def _(d):
        pl.semaphore_signal(barrier, inc=1, device_id=in_group(d)[1], device_id_type=MESH)

    @pl.loop(1, ns)
    def _(d):
        pl.semaphore_signal(barrier, inc=1, device_id=in_samples(d)[1], device_id_type=MESH)

    def grid(height, width):
        return (lax.broadcasted_iota(jnp.int32, (height, width), 0),
                lax.broadcasted_iota(jnp.int32, (height, width), 1))

    def hot(cond):
        return jnp.where(cond, 1.0, 0.0).astype(BF)

    def constants():
        r, c = grid(256, 256)
        pm[...] = hot((r // 32 == lax.rem(c, 8)) & (lax.rem(r, 32) == c // 8))
        r, c = grid(LANES, LANES)
        side = lax.rem(c, 2)
        for x in range(5):
            pe[x * LANES:(x + 1) * LANES] = hot(
                (c // 16 == x) & (((r == LANES - 1) & (side == 0)) | ((r == 0) & (side == 1))))
        r, c = grid(LANES, 256)
        near = hot(((c < LANES) & (c == r + 1)) | ((c >= LANES) & (c == r + LANES - 1)))
        r2 = lax.rem(r, 2)
        ends = ((r2 == 0) & (c == 0)) | ((r2 == 1) & (c == 255))
        for x in range(5):
            ps[x, 0:LANES] = near
            ps[x, LANES:256] = hot((r // 16 == x) & ends)

    def rows_in(s, v):
        slab = jnp.concatenate([v[x].reshape(256, LANES) for x in range(5)], axis=1)
        moved = jnp.dot(pm[...], slab, preferred_element_type=F32).astype(BF)
        for x in range(5):
            s[1, 1 + x] = moved[:, x * LANES:(x + 1) * LANES]

    def edges(s, f):
        slab = jnp.concatenate([s[1, 1 + x] for x in range(5)], axis=1)
        picked = jnp.dot(slab, pe[...], preferred_element_type=F32)
        acc = jnp.zeros((32, LANES), F32)
        for y in range(8):
            acc = jnp.where(level == y, picked[y * 32:(y + 1) * 32], acc)
        eo[f] = jnp.where(lane < 80, acc, 0.0).astype(BF)

    def halo(s, f):
        plan = (
            (2, eo.at[f], ei.at[f, 1], (smp, gx, other)),
            (3, eo.at[f], ei.at[f, 2], (smp, left, other)),
            (4, eo.at[f], ei.at[f, 0], (smp, right, other)),
            (0, s.at[1, 1], s.at[1, 6], (smp, left, gz)),
            (1, s.at[1, 5], s.at[1, 0], (smp, right, gz)),
        )
        return [
            pltpu.make_async_remote_copy(
                src_ref=src, dst_ref=dst, send_sem=hs.at[f, i], recv_sem=hr.at[f, i],
                device_id=dev, device_id_type=MESH,
            )
            for i, src, dst, dev in plan
        ]

    def shift(s, f):
        spread = []
        for i in range(3):
            e = ei[f, i].astype(F32)
            spread.append(jnp.concatenate([jnp.where(level == y, e, 0.0) for y in range(8)], axis=0).astype(BF))
        for slot in (1, 2, 3, 4, 5, 0, 6):
            which, x = (0, 4) if slot == 0 else (2, 0) if slot == 6 else (1, slot - 1)
            wide = jnp.concatenate([s[1, slot], spread[which]], axis=1)
            moved = jnp.dot(wide, ps[x], preferred_element_type=F32).astype(BF)
            s[0, slot] = moved[:, :LANES]
            s[2, slot] = moved[:, LANES:]

    def banded(dst, tap):
        zero = jnp.zeros((32, LANES), F32)
        for k in range(9):
            a, c = k // 3, k % 3
            base = jnp.concatenate(tap(a, c) + [jnp.zeros((32, 32), F32)], axis=1)
            r = [pltpu.roll(base, (32 * (m + 3)) % LANES, 1) if m != 1 else base for m in range(4)]
            low, mid_, top = lane < 32, lane < 64, lane >= 96
            tiles = (
                (jnp.where(mid_, r[0], 0.0), zero),
                (r[1], zero),
                (r[2], zero),
                (jnp.where(mid_, 0.0, r[3]), jnp.where(low, r[3], 0.0)),
                (jnp.where(top, r[0], 0.0), jnp.where(mid_, r[0], 0.0)),
                (zero, r[1]),
                (zero, r[2]),
                (zero, jnp.where(mid_, 0.0, r[3])),
            )
            for y, pair in enumerate(tiles):
                for t in range(2):
                    dst[k, y * 32:(y + 1) * 32, t * LANES:(t + 1) * LANES] = pair[t].astype(BF)

    def conv(w, s, xs):
        lhs = jnp.concatenate([w[k] for k in range(9)], axis=1)
        rhs = jnp.concatenate(
            [jnp.concatenate([s[k % 3, x + k // 3] for x in xs], axis=1) for k in range(9)], axis=0)
        return jnp.dot(lhs, rhs, preferred_element_type=F32)

    def diagonal(g):
        t = [[g[y * 32:(y + 1) * 32, u * LANES:(u + 1) * LANES] for u in range(2)] for y in range(8)]
        x0 = jnp.where(lane < 64, t[0][0] + t[4][1], jnp.where(lane >= 96, t[4][0], 0.0))
        x1 = t[1][0] + t[5][1]
        x2 = t[2][0] + t[6][1]
        x3 = jnp.where(lane >= 64, t[3][0] + t[7][1], jnp.where(lane < 32, t[3][1], 0.0))
        total = pltpu.roll(x0, 32, 1) + x1 + pltpu.roll(x2, 96, 1) + pltpu.roll(x3, 64, 1)
        return jnp.where(lane < 96, total, 0.0)

    def column(ref):
        row = lax.broadcasted_iota(jnp.int32, (32, 32), 0)
        col = lax.broadcasted_iota(jnp.int32, (32, 32), 1)
        one = jnp.sum(jnp.where(row == col, jnp.broadcast_to(ref[...], (32, 32)), 0.0), axis=1, keepdims=True)
        return jnp.concatenate([one] * 8, axis=0)

    def taps(w):
        return lambda a, c: [w[a * 9 + b * 3 + c].astype(F32) for b in range(3)]

    def turned(w):
        def tap(a, c):
            wide = jnp.concatenate([w[(2 - a) * 9 + (2 - b) * 3 + 2 - c].astype(F32) for b in range(3)]
                                   + [jnp.zeros((32, 32), F32)], axis=1)
            tall = wide.T
            return [tall[b * 32:(b + 1) * 32] for b in range(3)]
        return tap

    constants()
    for m in load_f:
        m.wait()
    rows_in(sf, vf)
    edges(sf, 0)
    pl.semaphore_wait(barrier, ng + ns - 2)
    moves_f = halo(sf, 0)
    for m in moves_f:
        m.start()
    for m in load_c:
        m.wait()
    rows_in(sc, vc)
    edges(sc, 1)
    moves_c = halo(sc, 1)
    for m in moves_c:
        m.start()
    for m in load_w:
        m.wait()

    banded(wa, taps(w1))
    banded(wv, turned(w2))
    banded(wb, taps(w2))

    def folded(v):
        total = v[0:32]
        for y in range(1, 8):
            total = total + v[y * 32:(y + 1) * 32]
        return jnp.sum(total, axis=1, keepdims=True)

    csum = jnp.zeros((256, LANES), F32)
    for x in range(5):
        csum = csum + sc[1, 1 + x].astype(F32)
    csum = folded(csum)

    def split(v, which):
        both = v + pltpu.roll(v, LANES - 2, 1)
        high = both.astype(BF).astype(F32)
        lanes = lax.broadcasted_iota(jnp.int32, v.shape, 1)
        pair = jnp.where(lanes < 2, high, pltpu.roll(both - high, 2, 1))
        return jnp.where(which & (lanes < 4), pair, v).astype(BF)

    for m in moves_f:
        m.wait_recv()
    shift(sf, 0)
    tiles = ((0, 1), (2, 3), (4,))
    bias = column(b1)
    for xs in tiles:
        v = conv(wa, sf, xs) + bias
        q = 1.0 / (1.0 + jnp.exp(-v))
        h = (v * q).astype(BF)
        d = q * (1.0 + v * (1.0 - q))
        for i, x in enumerate(xs):
            sh[1, 1 + x] = h[:, i * LANES:(i + 1) * LANES]
            dd[x] = d[:, i * LANES:(i + 1) * LANES]
    edges(sh, 2)
    moves_h = halo(sh, 2)
    for m in moves_h:
        m.start()

    for m in moves_c:
        m.wait_recv()
    shift(sc, 1)
    sums = jnp.zeros((256, LANES), F32)
    for xs in tiles:
        u = conv(wv, sc, xs)
        for i, x in enumerate(xs):
            p = (u[:, i * LANES:(i + 1) * LANES] * dd[x]).astype(BF)
            pg[x] = p
            sums = sums + p.astype(F32)

    def spans(s, c, a):
        return jnp.concatenate([s[c, a + x] for x in range(5)], axis=1)

    def nt(p, r):
        return lax.dot_general(p, r, (((1,), (1,)), ((), ())), preferred_element_type=F32)

    for k in range(9):
        a, c = k // 3, k % 3
        upstream = jnp.concatenate([pg[x] for x in range(5)], axis=1)
        pay[k * 32:(k + 1) * 32] = diagonal(nt(upstream, spans(sf, c, a)))
    for k in range(9):
        a, c = k // 3, k % 3
        own = jnp.concatenate([sh[1, 1 + x] for x in range(5)], axis=1)
        pay[288 + k * 32:288 + (k + 1) * 32] = diagonal(nt(spans(sc, 2 - c, 2 - a), own))

    pay[576:608] = jnp.where(lane == 0, folded(sums), jnp.where(lane == 1, csum, 0.0))
    pay[608:640] = jnp.zeros((32, LANES), F32)

    def bias_rows(first):
        r = lax.broadcasted_iota(jnp.int32, (rows, LANES), 0) + first
        return (r >= 576) & (r < 608)

    for s in range(ng):
        part = pay[s * rows:(s + 1) * rows]
        if (s + 1) * rows > 576 and s * rows < 608:
            snd[s] = split(part, bias_rows(s * rows))
        else:
            snd[s] = part.astype(BF)

    def send_a(d):
        peer, dev = in_group(d)
        return pltpu.make_async_remote_copy(
            src_ref=snd.at[peer], dst_ref=ra.at[me], send_sem=as_.at[peer], recv_sem=ar.at[me],
            device_id=dev, device_id_type=MESH)

    def from_a(d):
        peer, dev = in_group(d)
        return pltpu.make_async_remote_copy(
            src_ref=snd.at[peer], dst_ref=ra.at[peer], send_sem=as_.at[peer], recv_sem=ar.at[peer],
            device_id=dev, device_id_type=MESH)

    @pl.loop(1, ng)
    def _(d):
        send_a(d).start()

    ra[me] = snd[me]

    for m in moves_h:
        m.wait_recv()
    shift(sh, 2)
    bias2 = column(b2)
    for xs in tiles:
        v = conv(wb, sh, xs) + bias2
        for i, x in enumerate(xs):
            r = (v[:, i * LANES:(i + 1) * LANES] + sf[1, 1 + x].astype(F32)).astype(BF)
            back = lax.dot_general(pm[...], r, (((0,), (0,)), ((), ())), preferred_element_type=F32)
            out[x] = back.astype(BF)

    @pl.loop(1, ng)
    def _(d):
        from_a(d).wait_recv()

    def total(ref, n):
        acc = ref[0].astype(F32)
        for s in range(1, n):
            acc = acc + ref[s].astype(F32)
        return acc

    mine = bias_rows(me * rows)
    mid[...] = split(total(ra, ng), mine)

    def send_b(d):
        peer, dev = in_samples(d)
        return pltpu.make_async_remote_copy(
            src_ref=mid, dst_ref=rb.at[smp], send_sem=bs.at[peer], recv_sem=br.at[smp],
            device_id=dev, device_id_type=MESH)

    def from_b(d):
        peer, dev = in_samples(d)
        return pltpu.make_async_remote_copy(
            src_ref=mid, dst_ref=rb.at[peer], send_sem=bs.at[peer], recv_sem=br.at[peer],
            device_id=dev, device_id_type=MESH)

    @pl.loop(1, ns)
    def _(d):
        send_b(d).start()

    rb[smp] = mid[...]

    @pl.loop(1, ns)
    def _(d):
        from_b(d).wait_recv()

    fin[...] = split(total(rb, ns) * scale, mine)

    def send_c(d):
        peer, dev = in_group(d)
        return pltpu.make_async_remote_copy(
            src_ref=fin, dst_ref=rc.at[me], send_sem=cs.at[peer], recv_sem=cr.at[me],
            device_id=dev, device_id_type=MESH)

    def from_c(d):
        peer, dev = in_group(d)
        return pltpu.make_async_remote_copy(
            src_ref=fin, dst_ref=rc.at[peer], send_sem=cs.at[peer], recv_sem=cr.at[peer],
            device_id=dev, device_id_type=MESH)

    @pl.loop(1, ng)
    def _(d):
        send_c(d).start()

    rc[me] = fin[...]

    @pl.loop(1, ng)
    def _(d):
        from_c(d).wait_recv()

    for m in moves_f + moves_c + moves_h:
        m.wait_send()

    @pl.loop(1, ng)
    def _(d):
        send_a(d).wait_send()

    @pl.loop(1, ns)
    def _(d):
        send_b(d).wait_send()

    @pl.loop(1, ng)
    def _(d):
        send_c(d).wait_send()


def unpack(rows, rc, mid, out, g1, gb1, g2, gb2, pay, sem):
    moves = [pltpu.make_async_copy(mid.at[x], out.at[:, x], sem.at[x]) for x in range(5)]
    for m in moves:
        m.start()
    for s in range(PAY // rows):
        pay[s * rows:(s + 1) * rows] = rc[s].astype(F32)
    for base, ref in ((0, g1), (288, g2)):
        for k in range(9):
            a, c = k // 3, k % 3
            blk = pay[base + k * 32:base + (k + 1) * 32]
            for b in range(3):
                ref[a * 9 + b * 3 + c] = blk[:, b * 32:(b + 1) * 32]
    tail = pay[576:608]
    tail = tail + pltpu.roll(tail, LANES - 2, 1)
    row = lax.broadcasted_iota(jnp.int32, (32, 32), 0)
    col = lax.broadcasted_iota(jnp.int32, (32, 32), 1)
    for i, ref in ((0, gb1), (1, gb2)):
        ref[...] = jnp.sum(jnp.where(row == col, tail[:, i:i + 1], 0.0), axis=0, keepdims=True)
    for m in moves:
        m.wait()


def solution(mesh):
    sizes = tuple(mesh.shape[n] for n in ("smp", "gx", "gz"))
    ns, nx, nz = sizes
    ng = nx * nz
    rows = PAY // ng

    def shards(features, first_weight, first_bias, second_weight, second_bias, cotangent):
        cells = ns * nx * nz * 5 * 8 * LANES
        w1 = first_weight.transpose(1, 2, 3, 0, 4).reshape(27, 32, 32)
        w2 = second_weight.transpose(1, 2, 3, 0, 4).reshape(27, 32, 32)
        vm = pl.BlockSpec(memory_space=pltpu.VMEM)
        hbm = pl.BlockSpec(memory_space=pltpu.MemorySpace.HBM)
        dma = pltpu.SemaphoreType.DMA
        gathered, mid = pl.pallas_call(
            functools.partial(kernel, sizes, cells ** -0.5),
            out_shape=(
                jax.ShapeDtypeStruct((ng, rows, LANES), BF),
                jax.ShapeDtypeStruct((5, 256, LANES), BF),
            ),
            in_specs=[hbm] * 6,
            out_specs=(vm,) * 2,
            scratch_shapes=[
                pltpu.VMEM((5, 32, 8, LANES), BF),
                pltpu.VMEM((5, 32, 8, LANES), BF),
                pltpu.VMEM((27, 32, 32), BF),
                pltpu.VMEM((27, 32, 32), BF),
                pltpu.VMEM((1, 32), F32),
                pltpu.VMEM((1, 32), F32),
                pltpu.VMEM((256, 256), BF),
                pltpu.VMEM((640, LANES), BF),
                pltpu.VMEM((5, 256, 256), BF),
                pltpu.VMEM((3, 7, 256, LANES), BF),
                pltpu.VMEM((3, 7, 256, LANES), BF),
                pltpu.VMEM((3, 7, 256, LANES), BF),
                pltpu.VMEM((3, 32, LANES), BF),
                pltpu.VMEM((3, 3, 32, LANES), BF),
                pltpu.VMEM((9, 256, 256), BF),
                pltpu.VMEM((9, 256, 256), BF),
                pltpu.VMEM((9, 256, 256), BF),
                pltpu.VMEM((5, 256, LANES), F32),
                pltpu.VMEM((5, 256, LANES), BF),
                pltpu.VMEM((PAY, LANES), F32),
                pltpu.VMEM((ng, rows, LANES), BF),
                pltpu.VMEM((ng, rows, LANES), BF),
                pltpu.VMEM((rows, LANES), BF),
                pltpu.VMEM((ns, rows, LANES), BF),
                pltpu.VMEM((rows, LANES), BF),
                dma((14,)), dma((3, 5)), dma((3, 5)),
                dma((ng,)), dma((ng,)), dma((ns,)), dma((ns,)), dma((ng,)), dma((ng,)),
            ],
            compiler_params=pltpu.CompilerParams(
                collective_id=0, has_side_effects=True, vmem_limit_bytes=32 << 20),
        )(*(pltpu.with_memory_space_constraint(v, pltpu.MemorySpace.HBM) for v in (
            features[0], cotangent[0], w1, w2, first_bias.reshape(1, 32), second_bias.reshape(1, 32))))
        output, g1, gb1, g2, gb2 = pl.pallas_call(
            functools.partial(unpack, rows),
            out_shape=(
                jax.ShapeDtypeStruct((32, 5, 8, LANES), BF),
                jax.ShapeDtypeStruct((27, 32, 32), F32),
                jax.ShapeDtypeStruct((1, 32), F32),
                jax.ShapeDtypeStruct((27, 32, 32), F32),
                jax.ShapeDtypeStruct((1, 32), F32),
            ),
            in_specs=[vm] * 2,
            out_specs=(hbm, vm, vm, vm, vm),
            scratch_shapes=[pltpu.VMEM((PAY, LANES), F32), dma((5,))],
            compiler_params=pltpu.CompilerParams(vmem_limit_bytes=16 << 20),
        )(gathered, mid.reshape(5, 32, 8, LANES))
        back = lambda g: g.reshape(3, 3, 3, 32, 32).transpose(3, 0, 1, 2, 4)
        return output[None], back(g1), gb1.reshape(32), back(g2), gb2.reshape(32)

    block = P("smp", None, "gx", None, "gz")
    return jax.shard_map(
        shards, mesh=mesh, in_specs=(block, P(), P(), P(), P(), block),
        out_specs=(block, P(), P(), P(), P()), check_vma=False)
```

```python
import functools

import jax
import jax.numpy as jnp
from jax import lax
from jax.experimental import pallas as pl
from jax.experimental.pallas import tpu as pltpu
from jax.sharding import PartitionSpec as P

MESH = pl.DeviceIdType.MESH
BF = jnp.bfloat16
F32 = jnp.float32
LANES = 128
PAY = 448


def kernel(sizes, scale, feat, cot, w1h, w2h, b1h, b2h, rc, out,
           vf, vc, w1, w2, b1, b2, pm, pe, ps,
           sf, sc, sh, eo, ei, wa, wb, wv, dd, pg, pay, pk, snd, ra, mid, rb, fin,
           ins, hs, hr, as_, ar, bs, br, cs, cr):
    ns, nx, nz = sizes
    hx = min(4, nx)
    nlo = nx // hx
    nzt, ny = nz * nlo, ns // 2
    nr, na = 2 * hx, ny * nzt
    rows = PAY // nr
    smp, gx, gz = lax.axis_index("smp"), lax.axis_index("gx"), lax.axis_index("gz")
    left, right = lax.rem(gx + nx - 1, nx), lax.rem(gx + 1, nx)
    other = 1 - gz
    x_at, z_at = lax.rem(gx, hx), gz * nlo + gx // hx
    y_at, c_at = smp // 2, lax.rem(smp, 2)
    lane = lax.broadcasted_iota(jnp.int32, (32, LANES), 1)
    level = lax.rem(lane // 2, 8)

    def device(x, y, z, c):
        return (y * 2 + c, lax.rem(z, nlo) * hx + x, z // nlo)

    def far(n, m):
        return [(i, j) for i in range(n) for j in range(m) if i or j]

    me_r, me_a = x_at * 2 + c_at, y_at * nzt + z_at
    peers_r, peers_a = [], []
    for i, j in sorted(far(hx, 2), key=lambda o: -2 * min(o[0], hx - o[0]) - o[1]):
        x, c = lax.rem(x_at + i, hx), lax.rem(c_at + j, 2)
        peers_r.append((x * 2 + c, device(x, y_at, z_at, c)))
    for i, j in sorted(far(ny, nzt), key=lambda o: -min(o[0], ny - o[0]) - min(o[1], nzt - o[1])):
        y, z = lax.rem(y_at + i, ny), lax.rem(z_at + j, nzt)
        peers_a.append((y * nzt + z, device(x_at, y, z, c_at)))
    near = ((smp, gx, other), (smp, left, other), (smp, right, other), (smp, left, gz), (smp, right, gz))

    load_f = [pltpu.make_async_copy(feat.at[:, x], vf.at[x], ins.at[x]) for x in range(5)]
    load_c = [pltpu.make_async_copy(cot.at[:, x], vc.at[x], ins.at[5 + x]) for x in range(5)]
    load_w = [
        pltpu.make_async_copy(src, dst, ins.at[10 + i])
        for i, (src, dst) in enumerate(((w1h, w1), (w2h, w2), (b1h, b1), (b2h, b2)))
    ]
    for m in load_f + load_c + load_w:
        m.start()

    barrier = pltpu.get_barrier_semaphore()
    known = [dev for _, dev in peers_r] + [dev for _, dev in peers_a] + list(near)
    for dev in known:
        pl.semaphore_signal(barrier, inc=1, device_id=dev, device_id_type=MESH)

    def grid(height, width):
        return (lax.broadcasted_iota(jnp.int32, (height, width), 0),
                lax.broadcasted_iota(jnp.int32, (height, width), 1))

    def hot(cond):
        return jnp.where(cond, 1.0, 0.0).astype(BF)

    def first_constants():
        r, c = grid(256, 256)
        pm[...] = hot((r // 32 == lax.rem(c, 8)) & (lax.rem(r, 32) == c // 8))
        r, c = grid(LANES, LANES)
        side = lax.rem(c, 2)
        for x in range(5):
            pe[x * LANES:(x + 1) * LANES] = hot(
                (c // 16 == x) & (((r == LANES - 1) & (side == 0)) | ((r == 0) & (side == 1))))

    def later_constants():
        r, c = grid(LANES, 256)
        beside = hot(((c < LANES) & (c == r + 1)) | ((c >= LANES) & (c == r + LANES - 1)))
        r2 = lax.rem(r, 2)
        ends = ((r2 == 0) & (c == 0)) | ((r2 == 1) & (c == 255))
        for x in range(5):
            ps[x, 0:LANES] = beside
            ps[x, LANES:256] = hot((r // 16 == x) & ends)

    def rows_in(s, v):
        slab = jnp.concatenate([v[x].reshape(256, LANES) for x in range(5)], axis=1)
        moved = jnp.dot(pm[...], slab, preferred_element_type=F32).astype(BF)
        for x in range(5):
            s[1, 1 + x] = moved[:, x * LANES:(x + 1) * LANES]

    def edges(s, f):
        slab = jnp.concatenate([s[1, 1 + x] for x in range(5)], axis=1)
        picked = jnp.dot(slab, pe[...], preferred_element_type=F32)
        acc = jnp.zeros((32, LANES), F32)
        for y in range(8):
            acc = jnp.where(level == y, picked[y * 32:(y + 1) * 32], acc)
        eo[f] = jnp.where(lane < 80, acc, 0.0).astype(BF)

    def halo(s, f):
        plan = (
            (2, eo.at[f], ei.at[f, 1], near[0]),
            (3, eo.at[f], ei.at[f, 2], near[1]),
            (4, eo.at[f], ei.at[f, 0], near[2]),
            (0, s.at[1, 1], s.at[1, 6], near[3]),
            (1, s.at[1, 5], s.at[1, 0], near[4]),
        )
        return [
            pltpu.make_async_remote_copy(
                src_ref=src, dst_ref=dst, send_sem=hs.at[f, i], recv_sem=hr.at[f, i],
                device_id=dev, device_id_type=MESH,
            )
            for i, src, dst, dev in plan
        ]

    def shift(s, f):
        spread = []
        for i in range(3):
            e = ei[f, i].astype(F32)
            spread.append(jnp.concatenate([jnp.where(level == y, e, 0.0) for y in range(8)], axis=0).astype(BF))
        for slot in (1, 2, 3, 4, 5, 0, 6):
            which, x = (0, 4) if slot == 0 else (2, 0) if slot == 6 else (1, slot - 1)
            wide = jnp.concatenate([s[1, slot], spread[which]], axis=1)
            moved = jnp.dot(wide, ps[x], preferred_element_type=F32).astype(BF)
            s[0, slot] = moved[:, :LANES]
            s[2, slot] = moved[:, LANES:]

    def banded(dst, tap):
        zero = jnp.zeros((32, LANES), F32)
        for k in range(9):
            a, c = k // 3, k % 3
            base = jnp.concatenate(tap(a, c) + [jnp.zeros((32, 32), F32)], axis=1)
            r = [pltpu.roll(base, (32 * (m + 3)) % LANES, 1) if m != 1 else base for m in range(4)]
            low, mid_, top = lane < 32, lane < 64, lane >= 96
            tiles = (
                (jnp.where(mid_, r[0], 0.0), zero),
                (r[1], zero),
                (r[2], zero),
                (jnp.where(mid_, 0.0, r[3]), jnp.where(low, r[3], 0.0)),
                (jnp.where(top, r[0], 0.0), jnp.where(mid_, r[0], 0.0)),
                (zero, r[1]),
                (zero, r[2]),
                (zero, jnp.where(mid_, 0.0, r[3])),
            )
            for y, pair in enumerate(tiles):
                for t in range(2):
                    dst[k, y * 32:(y + 1) * 32, t * LANES:(t + 1) * LANES] = pair[t].astype(BF)

    def conv(w, s, xs):
        lhs = jnp.concatenate([w[k] for k in range(9)], axis=1)
        rhs = jnp.concatenate(
            [jnp.concatenate([s[k % 3, x + k // 3] for x in xs], axis=1) for k in range(9)], axis=0)
        return jnp.dot(lhs, rhs, preferred_element_type=F32)

    def diagonal(g):
        t = [[g[y * 32:(y + 1) * 32, u * LANES:(u + 1) * LANES] for u in range(2)] for y in range(8)]
        x0 = jnp.where(lane < 64, t[0][0] + t[4][1], jnp.where(lane >= 96, t[4][0], 0.0))
        x1 = t[1][0] + t[5][1]
        x2 = t[2][0] + t[6][1]
        x3 = jnp.where(lane >= 64, t[3][0] + t[7][1], jnp.where(lane < 32, t[3][1], 0.0))
        total = pltpu.roll(x0, 32, 1) + x1 + pltpu.roll(x2, 96, 1) + pltpu.roll(x3, 64, 1)
        return jnp.where(lane < 96, total, 0.0)

    def column(ref):
        row = lax.broadcasted_iota(jnp.int32, (32, 32), 0)
        col = lax.broadcasted_iota(jnp.int32, (32, 32), 1)
        one = jnp.sum(jnp.where(row == col, jnp.broadcast_to(ref[...], (32, 32)), 0.0), axis=1, keepdims=True)
        return jnp.concatenate([one] * 8, axis=0)

    def taps(w):
        return lambda a, c: [w[a * 9 + b * 3 + c].astype(F32) for b in range(3)]

    def turned(w):
        def tap(a, c):
            wide = jnp.concatenate([w[(2 - a) * 9 + (2 - b) * 3 + 2 - c].astype(F32) for b in range(3)]
                                   + [jnp.zeros((32, 32), F32)], axis=1)
            tall = wide.T
            return [tall[b * 32:(b + 1) * 32] for b in range(3)]
        return tap

    first_constants()
    for m in load_f:
        m.wait()
    rows_in(sf, vf)
    edges(sf, 0)
    for m in load_c:
        m.wait()
    rows_in(sc, vc)
    edges(sc, 1)
    pl.semaphore_wait(barrier, len(known))
    moves_f = halo(sf, 0)
    moves_c = halo(sc, 1)
    for m in moves_f[:3] + moves_c[:3] + moves_f[3:] + moves_c[3:]:
        m.start()
    later_constants()
    for m in load_w:
        m.wait()

    banded(wa, taps(w1))
    banded(wv, turned(w2))
    banded(wb, taps(w2))

    def folded(v):
        total = v[0:32]
        for y in range(1, 8):
            total = total + v[y * 32:(y + 1) * 32]
        return jnp.sum(total, axis=1, keepdims=True)

    csum = jnp.zeros((256, LANES), F32)
    for x in range(5):
        csum = csum + sc[1, 1 + x].astype(F32)
    csum = folded(csum)

    def split(v, which):
        both = v + pltpu.roll(v, LANES - 2, 1)
        high = both.astype(BF).astype(F32)
        lanes = lax.broadcasted_iota(jnp.int32, v.shape, 1)
        pair = jnp.where(lanes < 98, high, pltpu.roll(both - high, 2, 1))
        return jnp.where(which & (lanes >= 96) & (lanes < 100), pair, v).astype(BF)

    for m in moves_f:
        m.wait_recv()
    shift(sf, 0)
    tiles = ((0, 1), (2, 3), (4,))
    bias = column(b1)
    for xs in tiles:
        v = conv(wa, sf, xs) + bias
        q = 1.0 / (1.0 + jnp.exp(-v))
        h = (v * q).astype(BF)
        d = q * (1.0 + v * (1.0 - q))
        for i, x in enumerate(xs):
            sh[1, 1 + x] = h[:, i * LANES:(i + 1) * LANES]
            dd[x] = d[:, i * LANES:(i + 1) * LANES]
    edges(sh, 2)
    moves_h = halo(sh, 2)
    for m in moves_h:
        m.start()

    for m in moves_c:
        m.wait_recv()
    shift(sc, 1)
    sums = jnp.zeros((256, LANES), F32)
    for xs in tiles:
        u = conv(wv, sc, xs)
        for i, x in enumerate(xs):
            p = (u[:, i * LANES:(i + 1) * LANES] * dd[x]).astype(BF)
            pg[x] = p
            sums = sums + p.astype(F32)

    def spans(s, c, a):
        return jnp.concatenate([s[c, a + x] for x in range(5)], axis=1)

    def nt(p, r):
        return lax.dot_general(p, r, (((1,), (1,)), ((), ())), preferred_element_type=F32)

    for k in range(9):
        a, c = k // 3, k % 3
        upstream = jnp.concatenate([pg[x] for x in range(5)], axis=1)
        pay[k * 32:(k + 1) * 32] = diagonal(nt(upstream, spans(sf, c, a)))
    for k in range(9):
        a, c = k // 3, k % 3
        own = jnp.concatenate([sh[1, 1 + x] for x in range(5)], axis=1)
        pay[288 + k * 32:288 + (k + 1) * 32] = diagonal(nt(spans(sc, 2 - c, 2 - a), own))

    biases = jnp.where(lane == 96, folded(sums), jnp.where(lane == 97, csum, 0.0))
    for n in range(14):
        g, j = n // 3, n % 3
        if n < 12:
            extra = pltpu.roll(pay[(4 * g + 3) * 32:(4 * g + 4) * 32], 96 - 32 * j, 1)
            part = jnp.where(lane < 96, pay[(4 * g + j) * 32:(4 * g + j + 1) * 32], extra)
        else:
            part = pay[(n + 4) * 32:(n + 5) * 32]
            if n == 13:
                part = part + biases
        pk[n * 32:(n + 1) * 32] = part

    def bias_rows(first):
        r = lax.broadcasted_iota(jnp.int32, (rows, LANES), 0) + first
        return r >= PAY - 32

    for s in range(nr):
        part = pk[s * rows:(s + 1) * rows]
        snd[s] = split(part, bias_rows(s * rows)) if (s + 1) * rows > PAY - 32 else part.astype(BF)

    def remote(src, dst, send, recv, dev):
        return pltpu.make_async_remote_copy(
            src_ref=src, dst_ref=dst, send_sem=send, recv_sem=recv, device_id=dev, device_id_type=MESH)

    out_a = [remote(snd.at[p], ra.at[me_r], as_.at[p], ar.at[me_r], dev) for p, dev in peers_r]
    in_a = [remote(snd.at[p], ra.at[p], as_.at[p], ar.at[p], dev) for p, dev in peers_r]
    out_b = [remote(mid, rb.at[me_a], bs.at[p], br.at[me_a], dev) for p, dev in peers_a]
    in_b = [remote(mid, rb.at[p], bs.at[p], br.at[p], dev) for p, dev in peers_a]
    out_c = [remote(fin, rc.at[me_r], cs.at[p], cr.at[me_r], dev) for p, dev in peers_r]
    in_c = [remote(fin, rc.at[p], cs.at[p], cr.at[p], dev) for p, dev in peers_r]

    for m in out_a:
        m.start()
    ra[me_r] = snd[me_r]

    def total(ref, n):
        acc = ref[0].astype(F32)
        for s in range(1, n):
            acc = acc + ref[s].astype(F32)
        return acc

    for m in moves_h:
        m.wait_recv()
    shift(sh, 2)
    bias2 = column(b2)

    def finish(xs):
        v = conv(wb, sh, xs) + bias2
        for i, x in enumerate(xs):
            r = (v[:, i * LANES:(i + 1) * LANES] + sf[1, 1 + x].astype(F32)).astype(BF)
            back = lax.dot_general(pm[...], r, (((0,), (0,)), ((), ())), preferred_element_type=F32)
            out[x] = back.astype(BF)

    finish(tiles[0])
    for m in in_a:
        m.wait_recv()
    mine = bias_rows(me_r * rows)
    mid[...] = split(total(ra, nr), mine)
    for m in out_b:
        m.start()
    rb[me_a] = mid[...]
    finish(tiles[1])
    finish(tiles[2])
    for m in in_b:
        m.wait_recv()
    fin[...] = split(total(rb, na) * scale, mine)
    for m in out_c:
        m.start()
    rc[me_r] = fin[...]
    for m in moves_f + moves_c + moves_h + out_a + out_b:
        m.wait_send()
    for m in in_c:
        m.wait_recv()
    for m in out_c:
        m.wait_send()

def unpack(rows, rc, mid, out, g1, gb1, g2, gb2, pay, sem):
    moves = [pltpu.make_async_copy(mid.at[x], out.at[:, x], sem.at[x]) for x in range(5)]
    for m in moves:
        m.start()
    for s in range(PAY // rows):
        pay[s * rows:(s + 1) * rows] = rc[s].astype(F32)
    for n in range(18):
        ref, k = (g1, n) if n < 9 else (g2, n - 9)
        a, c = k // 3, k % 3
        for b in range(3):
            if n >= 16:
                block, place = n - 4, b
            elif n % 4 == 3:
                block, place = 3 * (n // 4) + b, 3
            else:
                block, place = 3 * (n // 4) + n % 4, b
            ref[a * 9 + b * 3 + c] = pay[block * 32:(block + 1) * 32, place * 32:(place + 1) * 32]
    tail = pay[PAY - 32:]
    tail = tail + pltpu.roll(tail, LANES - 2, 1)
    row = lax.broadcasted_iota(jnp.int32, (32, 32), 0)
    col = lax.broadcasted_iota(jnp.int32, (32, 32), 1)
    for i, ref in ((96, gb1), (97, gb2)):
        ref[...] = jnp.sum(jnp.where(row == col, tail[:, i:i + 1], 0.0), axis=0, keepdims=True)
    for m in moves:
        m.wait()


def solution(mesh):
    sizes = tuple(mesh.shape[n] for n in ("smp", "gx", "gz"))
    ns, nx, nz = sizes
    hx = min(4, nx)
    nr, na = 2 * hx, ns * nx * nz // (2 * hx)
    rows = PAY // nr

    def shards(features, first_weight, first_bias, second_weight, second_bias, cotangent):
        cells = ns * nx * nz * 5 * 8 * LANES
        w1 = first_weight.transpose(1, 2, 3, 0, 4).reshape(27, 32, 32)
        w2 = second_weight.transpose(1, 2, 3, 0, 4).reshape(27, 32, 32)
        vm = pl.BlockSpec(memory_space=pltpu.VMEM)
        hbm = pl.BlockSpec(memory_space=pltpu.MemorySpace.HBM)
        dma = pltpu.SemaphoreType.DMA
        gathered, mid = pl.pallas_call(
            functools.partial(kernel, sizes, cells ** -0.5),
            out_shape=(
                jax.ShapeDtypeStruct((nr, rows, LANES), BF),
                jax.ShapeDtypeStruct((5, 256, LANES), BF),
            ),
            in_specs=[hbm] * 6,
            out_specs=(vm,) * 2,
            scratch_shapes=[
                pltpu.VMEM((5, 32, 8, LANES), BF),
                pltpu.VMEM((5, 32, 8, LANES), BF),
                pltpu.VMEM((27, 32, 32), BF),
                pltpu.VMEM((27, 32, 32), BF),
                pltpu.VMEM((1, 32), F32),
                pltpu.VMEM((1, 32), F32),
                pltpu.VMEM((256, 256), BF),
                pltpu.VMEM((640, LANES), BF),
                pltpu.VMEM((5, 256, 256), BF),
                pltpu.VMEM((3, 7, 256, LANES), BF),
                pltpu.VMEM((3, 7, 256, LANES), BF),
                pltpu.VMEM((3, 7, 256, LANES), BF),
                pltpu.VMEM((3, 32, LANES), BF),
                pltpu.VMEM((3, 3, 32, LANES), BF),
                pltpu.VMEM((9, 256, 256), BF),
                pltpu.VMEM((9, 256, 256), BF),
                pltpu.VMEM((9, 256, 256), BF),
                pltpu.VMEM((5, 256, LANES), F32),
                pltpu.VMEM((5, 256, LANES), BF),
                pltpu.VMEM((576, LANES), F32),
                pltpu.VMEM((PAY, LANES), F32),
                pltpu.VMEM((nr, rows, LANES), BF),
                pltpu.VMEM((nr, rows, LANES), BF),
                pltpu.VMEM((rows, LANES), BF),
                pltpu.VMEM((na, rows, LANES), BF),
                pltpu.VMEM((rows, LANES), BF),
                dma((14,)), dma((3, 5)), dma((3, 5)),
                dma((nr,)), dma((nr,)), dma((na,)), dma((na,)), dma((nr,)), dma((nr,)),
            ],
            compiler_params=pltpu.CompilerParams(
                collective_id=0, has_side_effects=True, vmem_limit_bytes=32 << 20),
        )(*(pltpu.with_memory_space_constraint(v, pltpu.MemorySpace.HBM) for v in (
            features[0], cotangent[0], w1, w2, first_bias.reshape(1, 32), second_bias.reshape(1, 32))))
        output, g1, gb1, g2, gb2 = pl.pallas_call(
            functools.partial(unpack, rows),
            out_shape=(
                jax.ShapeDtypeStruct((32, 5, 8, LANES), BF),
                jax.ShapeDtypeStruct((27, 32, 32), F32),
                jax.ShapeDtypeStruct((1, 32), F32),
                jax.ShapeDtypeStruct((27, 32, 32), F32),
                jax.ShapeDtypeStruct((1, 32), F32),
            ),
            in_specs=[vm] * 2,
            out_specs=(hbm, vm, vm, vm, vm),
            scratch_shapes=[pltpu.VMEM((PAY, LANES), F32), dma((5,))],
            compiler_params=pltpu.CompilerParams(vmem_limit_bytes=16 << 20),
        )(gathered, mid.reshape(5, 32, 8, LANES))
        back = lambda g: g.reshape(3, 3, 3, 32, 32).transpose(3, 0, 1, 2, 4)
        return output[None], back(g1), gb1.reshape(32), back(g2), gb2.reshape(32)

    block = P("smp", None, "gx", None, "gz")
    return jax.shard_map(
        shards, mesh=mesh, in_specs=(block, P(), P(), P(), P(), block),
        out_specs=(block, P(), P(), P(), P()), check_vma=False)
```

```python
import functools

import jax
import jax.numpy as jnp
from jax import lax
from jax.experimental import pallas as pl
from jax.experimental.pallas import tpu as pltpu
from jax.sharding import PartitionSpec as P

MESH = pl.DeviceIdType.MESH
BF = jnp.bfloat16
F32 = jnp.float32
LANES = 128
PAY = 448


def kernel(sizes, scale, feat, cot, w1h, w2h, b1h, b2h, rc, out,
           vf, vc, w1, w2, b1, b2, pm, pe, ps,
           sf, sc, sh, eo, ei, wa, wb, wv, dd, pg, pay, pk, snd, ra, mid, rb, fin,
           ins, hs, hr, as_, ar, bs, br, cs, cr):
    ns, nx, nz = sizes
    hx = min(4, nx)
    nlo = nx // hx
    nzt, ny = nz * nlo, ns // 2
    nr, na = 2 * hx, ny * nzt
    rows = PAY // nr
    smp, gx, gz = lax.axis_index("smp"), lax.axis_index("gx"), lax.axis_index("gz")
    left, right = lax.rem(gx + nx - 1, nx), lax.rem(gx + 1, nx)
    other = 1 - gz
    x_at, z_at = lax.rem(gx, hx), gz * nlo + gx // hx
    y_at, c_at = smp // 2, lax.rem(smp, 2)
    lane = lax.broadcasted_iota(jnp.int32, (32, LANES), 1)
    level = lax.rem(lane // 2, 8)

    def device(x, y, z, c):
        return (y * 2 + c, lax.rem(z, nlo) * hx + x, z // nlo)

    def far(n, m):
        return [(i, j) for i in range(n) for j in range(m) if i or j]

    me_r, me_a = x_at * 2 + c_at, y_at * nzt + z_at
    peers_r, peers_a = [], []
    for i, j in sorted(far(hx, 2), key=lambda o: -2 * min(o[0], hx - o[0]) - o[1]):
        x, c = lax.rem(x_at + i, hx), lax.rem(c_at + j, 2)
        peers_r.append((x * 2 + c, device(x, y_at, z_at, c)))
    for i, j in sorted(far(ny, nzt), key=lambda o: -min(o[0], ny - o[0]) - min(o[1], nzt - o[1])):
        y, z = lax.rem(y_at + i, ny), lax.rem(z_at + j, nzt)
        peers_a.append((y * nzt + z, device(x_at, y, z, c_at)))
    near = ((smp, gx, other), (smp, left, other), (smp, right, other), (smp, left, gz), (smp, right, gz))

    load_f = [pltpu.make_async_copy(feat.at[:, x], vf.at[x], ins.at[x]) for x in range(5)]
    load_c = [pltpu.make_async_copy(cot.at[:, x], vc.at[x], ins.at[5 + x]) for x in range(5)]
    load_w = [
        pltpu.make_async_copy(src, dst, ins.at[10 + i])
        for i, (src, dst) in enumerate(((w1h, w1), (w2h, w2), (b1h, b1), (b2h, b2)))
    ]
    for m in load_f + load_c + load_w:
        m.start()

    barrier = pltpu.get_barrier_semaphore()
    known = [dev for _, dev in peers_r] + [dev for _, dev in peers_a] + list(near)
    for dev in known:
        pl.semaphore_signal(barrier, inc=1, device_id=dev, device_id_type=MESH)

    def grid(height, width):
        return (lax.broadcasted_iota(jnp.int32, (height, width), 0),
                lax.broadcasted_iota(jnp.int32, (height, width), 1))

    def hot(cond):
        return jnp.where(cond, 1.0, 0.0).astype(BF)

    def first_constants():
        r, c = grid(256, 256)
        pm[...] = hot((r // 32 == lax.rem(c, 8)) & (lax.rem(r, 32) == c // 8))
        r, c = grid(LANES, LANES)
        side = lax.rem(c, 2)
        for x in range(5):
            pe[x * LANES:(x + 1) * LANES] = hot(
                (c // 16 == x) & (((r == LANES - 1) & (side == 0)) | ((r == 0) & (side == 1))))

    def later_constants():
        r, c = grid(LANES, 256)
        beside = hot(((c < LANES) & (c == r + 1)) | ((c >= LANES) & (c == r + LANES - 1)))
        r2 = lax.rem(r, 2)
        ends = ((r2 == 0) & (c == 0)) | ((r2 == 1) & (c == 255))
        for x in range(5):
            ps[x, 0:LANES] = beside
            ps[x, LANES:256] = hot((r // 16 == x) & ends)

    def rows_in(s, v):
        slab = jnp.concatenate([v[x].reshape(256, LANES) for x in range(5)], axis=1)
        moved = jnp.dot(pm[...], slab, preferred_element_type=F32).astype(BF)
        for x in range(5):
            s[1, 1 + x] = moved[:, x * LANES:(x + 1) * LANES]

    def edges(s, f):
        slab = jnp.concatenate([s[1, 1 + x] for x in range(5)], axis=1)
        picked = jnp.dot(slab, pe[...], preferred_element_type=F32)
        acc = jnp.zeros((32, LANES), F32)
        for y in range(8):
            acc = jnp.where(level == y, picked[y * 32:(y + 1) * 32], acc)
        eo[f] = jnp.where(lane < 80, acc, 0.0).astype(BF)

    def halo(s, f):
        plan = (
            (2, eo.at[f], ei.at[f, 1], near[0]),
            (3, eo.at[f], ei.at[f, 2], near[1]),
            (4, eo.at[f], ei.at[f, 0], near[2]),
            (0, s.at[1, 1], s.at[1, 6], near[3]),
            (1, s.at[1, 5], s.at[1, 0], near[4]),
        )
        return [
            pltpu.make_async_remote_copy(
                src_ref=src, dst_ref=dst, send_sem=hs.at[f, i], recv_sem=hr.at[f, i],
                device_id=dev, device_id_type=MESH,
            )
            for i, src, dst, dev in plan
        ]

    def shift(s, f, slots):
        spread = {}
        for slot in slots:
            which, x = (0, 4) if slot == 0 else (2, 0) if slot == 6 else (1, slot - 1)
            if which not in spread:
                e = ei[f, which].astype(F32)
                spread[which] = jnp.concatenate(
                    [jnp.where(level == y, e, 0.0) for y in range(8)], axis=0).astype(BF)
            wide = jnp.concatenate([s[1, slot], spread[which]], axis=1)
            moved = jnp.dot(wide, ps[x], preferred_element_type=F32).astype(BF)
            s[0, slot] = moved[:, :LANES]
            s[2, slot] = moved[:, LANES:]

    def banded(dst, tap):
        zero = jnp.zeros((32, LANES), F32)
        for k in range(9):
            a, c = k // 3, k % 3
            base = jnp.concatenate(tap(a, c) + [jnp.zeros((32, 32), F32)], axis=1)
            r = [pltpu.roll(base, (32 * (m + 3)) % LANES, 1) if m != 1 else base for m in range(4)]
            low, mid_, top = lane < 32, lane < 64, lane >= 96
            tiles = (
                (jnp.where(mid_, r[0], 0.0), zero),
                (r[1], zero),
                (r[2], zero),
                (jnp.where(mid_, 0.0, r[3]), jnp.where(low, r[3], 0.0)),
                (jnp.where(top, r[0], 0.0), jnp.where(mid_, r[0], 0.0)),
                (zero, r[1]),
                (zero, r[2]),
                (zero, jnp.where(mid_, 0.0, r[3])),
            )
            for y, pair in enumerate(tiles):
                for t in range(2):
                    dst[k, y * 32:(y + 1) * 32, t * LANES:(t + 1) * LANES] = pair[t].astype(BF)

    def conv(w, s, xs):
        lhs = jnp.concatenate([w[k] for k in range(9)], axis=1)
        rhs = jnp.concatenate(
            [jnp.concatenate([s[k % 3, x + k // 3] for x in xs], axis=1) for k in range(9)], axis=0)
        return jnp.dot(lhs, rhs, preferred_element_type=F32)

    def diagonal(g):
        t = [[g[y * 32:(y + 1) * 32, u * LANES:(u + 1) * LANES] for u in range(2)] for y in range(8)]
        x0 = jnp.where(lane < 64, t[0][0] + t[4][1], jnp.where(lane >= 96, t[4][0], 0.0))
        x1 = t[1][0] + t[5][1]
        x2 = t[2][0] + t[6][1]
        x3 = jnp.where(lane >= 64, t[3][0] + t[7][1], jnp.where(lane < 32, t[3][1], 0.0))
        total = pltpu.roll(x0, 32, 1) + x1 + pltpu.roll(x2, 96, 1) + pltpu.roll(x3, 64, 1)
        return jnp.where(lane < 96, total, 0.0)

    def column(ref):
        row = lax.broadcasted_iota(jnp.int32, (32, 32), 0)
        col = lax.broadcasted_iota(jnp.int32, (32, 32), 1)
        one = jnp.sum(jnp.where(row == col, jnp.broadcast_to(ref[...], (32, 32)), 0.0), axis=1, keepdims=True)
        return jnp.concatenate([one] * 8, axis=0)

    def taps(w):
        return lambda a, c: [w[a * 9 + b * 3 + c].astype(F32) for b in range(3)]

    def turned(w):
        def tap(a, c):
            wide = jnp.concatenate([w[(2 - a) * 9 + (2 - b) * 3 + 2 - c].astype(F32) for b in range(3)]
                                   + [jnp.zeros((32, 32), F32)], axis=1)
            tall = wide.T
            return [tall[b * 32:(b + 1) * 32] for b in range(3)]
        return tap

    first_constants()
    for m in load_f:
        m.wait()
    rows_in(sf, vf)
    edges(sf, 0)
    for m in load_c:
        m.wait()
    rows_in(sc, vc)
    edges(sc, 1)
    pl.semaphore_wait(barrier, len(known))
    moves_f = halo(sf, 0)
    moves_c = halo(sc, 1)
    for m in moves_f[:3] + moves_c[:3] + moves_f[3:] + moves_c[3:]:
        m.start()
    later_constants()
    for m in load_w:
        m.wait()

    banded(wa, taps(w1))
    banded(wv, turned(w2))

    def folded(v):
        total = v[0:32]
        for y in range(1, 8):
            total = total + v[y * 32:(y + 1) * 32]
        return jnp.sum(total, axis=1, keepdims=True)

    csum = jnp.zeros((256, LANES), F32)
    for x in range(5):
        csum = csum + sc[1, 1 + x].astype(F32)
    csum = folded(csum)

    def split(v, which):
        both = v + pltpu.roll(v, LANES - 2, 1)
        high = both.astype(BF).astype(F32)
        lanes = lax.broadcasted_iota(jnp.int32, v.shape, 1)
        pair = jnp.where(lanes < 98, high, pltpu.roll(both - high, 2, 1))
        return jnp.where(which & (lanes >= 96) & (lanes < 100), pair, v).astype(BF)

    bias = column(b1)
    inner, outer = (1, 2, 3, 4, 5), (0, 6)
    tiles = ((1, 2), (3, 4), (0,))

    def forward(xs):
        v = conv(wa, sf, xs) + bias
        q = 1.0 / (1.0 + jnp.exp(-v))
        h = (v * q).astype(BF)
        d = q * (1.0 + v * (1.0 - q))
        for i, x in enumerate(xs):
            sh[1, 1 + x] = h[:, i * LANES:(i + 1) * LANES]
            dd[x] = d[:, i * LANES:(i + 1) * LANES]

    def backward(xs):
        u = conv(wv, sc, xs)
        part = jnp.zeros((256, LANES), F32)
        for i, x in enumerate(xs):
            p = (u[:, i * LANES:(i + 1) * LANES] * dd[x]).astype(BF)
            pg[x] = p
            part = part + p.astype(F32)
        return part

    for m in moves_f:
        m.wait_recv()
    shift(sf, 0, inner + outer)
    for xs in tiles:
        forward(xs)
    edges(sh, 2)
    moves_h = halo(sh, 2)
    for m in moves_h:
        m.start()
    for m in moves_c:
        m.wait_recv()
    shift(sc, 1, inner + outer)
    sums = jnp.zeros((256, LANES), F32)
    for xs in tiles:
        sums = sums + backward(xs)

    def spans(s, c, a):
        return jnp.concatenate([s[c, a + x] for x in range(5)], axis=1)

    def nt(p, r):
        return lax.dot_general(p, r, (((1,), (1,)), ((), ())), preferred_element_type=F32)

    for k in range(9):
        a, c = k // 3, k % 3
        upstream = jnp.concatenate([pg[x] for x in range(5)], axis=1)
        pay[k * 32:(k + 1) * 32] = diagonal(nt(upstream, spans(sf, c, a)))
    for k in range(9):
        a, c = k // 3, k % 3
        own = jnp.concatenate([sh[1, 1 + x] for x in range(5)], axis=1)
        pay[288 + k * 32:288 + (k + 1) * 32] = diagonal(nt(spans(sc, 2 - c, 2 - a), own))

    biases = jnp.where(lane == 96, folded(sums), jnp.where(lane == 97, csum, 0.0))
    for n in range(14):
        g, j = n // 3, n % 3
        if n < 12:
            extra = pltpu.roll(pay[(4 * g + 3) * 32:(4 * g + 4) * 32], 96 - 32 * j, 1)
            part = jnp.where(lane < 96, pay[(4 * g + j) * 32:(4 * g + j + 1) * 32], extra)
        else:
            part = pay[(n + 4) * 32:(n + 5) * 32]
            if n == 13:
                part = part + biases
        pk[n * 32:(n + 1) * 32] = part

    def bias_rows(first):
        r = lax.broadcasted_iota(jnp.int32, (rows, LANES), 0) + first
        return r >= PAY - 32

    for s in range(nr):
        part = pk[s * rows:(s + 1) * rows]
        snd[s] = split(part, bias_rows(s * rows)) if (s + 1) * rows > PAY - 32 else part.astype(BF)

    def remote(src, dst, send, recv, dev):
        return pltpu.make_async_remote_copy(
            src_ref=src, dst_ref=dst, send_sem=send, recv_sem=recv, device_id=dev, device_id_type=MESH)

    out_a = [remote(snd.at[p], ra.at[me_r], as_.at[p], ar.at[me_r], dev) for p, dev in peers_r]
    in_a = [remote(snd.at[p], ra.at[p], as_.at[p], ar.at[p], dev) for p, dev in peers_r]
    out_b = [remote(mid, rb.at[me_a], bs.at[p], br.at[me_a], dev) for p, dev in peers_a]
    in_b = [remote(mid, rb.at[p], bs.at[p], br.at[p], dev) for p, dev in peers_a]
    out_c = [remote(fin, rc.at[me_r], cs.at[p], cr.at[me_r], dev) for p, dev in peers_r]
    in_c = [remote(fin, rc.at[p], cs.at[p], cr.at[p], dev) for p, dev in peers_r]

    for m in out_a:
        m.start()
    ra[me_r] = snd[me_r]

    def total(ref, n):
        acc = ref[0].astype(F32)
        for s in range(1, n):
            acc = acc + ref[s].astype(F32)
        return acc

    banded(wb, taps(w2))
    bias2 = column(b2)

    def finish(xs):
        v = conv(wb, sh, xs) + bias2
        for i, x in enumerate(xs):
            r = (v[:, i * LANES:(i + 1) * LANES] + sf[1, 1 + x].astype(F32)).astype(BF)
            back = lax.dot_general(pm[...], r, (((0,), (0,)), ((), ())), preferred_element_type=F32)
            out[x] = back.astype(BF)

    for m in in_a:
        m.wait_recv()
    mine = bias_rows(me_r * rows)
    mid[...] = split(total(ra, nr), mine)
    for m in out_b:
        m.start()
    rb[me_a] = mid[...]
    for m in moves_h:
        m.wait_recv()
    shift(sh, 2, inner + outer)
    for xs in tiles:
        finish(xs)
    for m in in_b:
        m.wait_recv()
    fin[...] = split(total(rb, na) * scale, mine)
    for m in out_c:
        m.start()
    rc[me_r] = fin[...]
    for m in moves_f + moves_c + moves_h + out_a + out_b:
        m.wait_send()
    for m in in_c:
        m.wait_recv()
    for m in out_c:
        m.wait_send()

def unpack(rows, rc, mid, out, g1, gb1, g2, gb2, pay, v1, v2, vb, sem):
    moves = [pltpu.make_async_copy(mid.at[x], out.at[:, x], sem.at[x]) for x in range(5)]
    for m in moves:
        m.start()
    for s in range(PAY // rows):
        pay[s * rows:(s + 1) * rows] = rc[s].astype(F32)
    tail = pay[PAY - 32:]
    tail = tail + pltpu.roll(tail, LANES - 2, 1)
    row = lax.broadcasted_iota(jnp.int32, (32, 32), 0)
    col = lax.broadcasted_iota(jnp.int32, (32, 32), 1)

    def send(src, dst):
        moves.append(pltpu.make_async_copy(src, dst, sem.at[len(moves)]))
        moves[-1].start()

    for i, ref in enumerate((gb1, gb2)):
        vb[i] = jnp.sum(jnp.where(row == col, tail[:, 96 + i:97 + i], 0.0), axis=0, keepdims=True)
        send(vb.at[i], ref)
    for n in range(18):
        ref, k = (v1, n) if n < 9 else (v2, n - 9)
        a, c = k // 3, k % 3
        for b in range(3):
            if n >= 16:
                block, place = n - 4, b
            elif n % 4 == 3:
                block, place = 3 * (n // 4) + b, 3
            else:
                block, place = 3 * (n // 4) + n % 4, b
            ref[a * 9 + b * 3 + c] = pay[block * 32:(block + 1) * 32, place * 32:(place + 1) * 32]
        if c == 2:
            part = pl.ds(a * 9, 9)
            send(ref.at[part], (g1 if n < 9 else g2).at[part])
    for m in moves:
        m.wait()


def solution(mesh):
    sizes = tuple(mesh.shape[n] for n in ("smp", "gx", "gz"))
    ns, nx, nz = sizes
    hx = min(4, nx)
    nr, na = 2 * hx, ns * nx * nz // (2 * hx)
    rows = PAY // nr

    def shards(features, first_weight, first_bias, second_weight, second_bias, cotangent):
        cells = ns * nx * nz * 5 * 8 * LANES
        w1 = first_weight.transpose(1, 2, 3, 0, 4).reshape(27, 32, 32)
        w2 = second_weight.transpose(1, 2, 3, 0, 4).reshape(27, 32, 32)
        vm = pl.BlockSpec(memory_space=pltpu.VMEM)
        hbm = pl.BlockSpec(memory_space=pltpu.MemorySpace.HBM)
        dma = pltpu.SemaphoreType.DMA
        gathered, mid = pl.pallas_call(
            functools.partial(kernel, sizes, cells ** -0.5),
            out_shape=(
                jax.ShapeDtypeStruct((nr, rows, LANES), BF),
                jax.ShapeDtypeStruct((5, 256, LANES), BF),
            ),
            in_specs=[hbm] * 6,
            out_specs=(vm,) * 2,
            scratch_shapes=[
                pltpu.VMEM((5, 32, 8, LANES), BF),
                pltpu.VMEM((5, 32, 8, LANES), BF),
                pltpu.VMEM((27, 32, 32), BF),
                pltpu.VMEM((27, 32, 32), BF),
                pltpu.VMEM((1, 32), F32),
                pltpu.VMEM((1, 32), F32),
                pltpu.VMEM((256, 256), BF),
                pltpu.VMEM((640, LANES), BF),
                pltpu.VMEM((5, 256, 256), BF),
                pltpu.VMEM((3, 7, 256, LANES), BF),
                pltpu.VMEM((3, 7, 256, LANES), BF),
                pltpu.VMEM((3, 7, 256, LANES), BF),
                pltpu.VMEM((3, 32, LANES), BF),
                pltpu.VMEM((3, 3, 32, LANES), BF),
                pltpu.VMEM((9, 256, 256), BF),
                pltpu.VMEM((9, 256, 256), BF),
                pltpu.VMEM((9, 256, 256), BF),
                pltpu.VMEM((5, 256, LANES), F32),
                pltpu.VMEM((5, 256, LANES), BF),
                pltpu.VMEM((576, LANES), F32),
                pltpu.VMEM((PAY, LANES), F32),
                pltpu.VMEM((nr, rows, LANES), BF),
                pltpu.VMEM((nr, rows, LANES), BF),
                pltpu.VMEM((rows, LANES), BF),
                pltpu.VMEM((na, rows, LANES), BF),
                pltpu.VMEM((rows, LANES), BF),
                dma((14,)), dma((3, 5)), dma((3, 5)),
                dma((nr,)), dma((nr,)), dma((na,)), dma((na,)), dma((nr,)), dma((nr,)),
            ],
            compiler_params=pltpu.CompilerParams(
                collective_id=0, has_side_effects=True, vmem_limit_bytes=32 << 20),
        )(*(pltpu.with_memory_space_constraint(v, pltpu.MemorySpace.HBM) for v in (
            features[0], cotangent[0], w1, w2, first_bias.reshape(1, 32), second_bias.reshape(1, 32))))
        output, g1, gb1, g2, gb2 = pl.pallas_call(
            functools.partial(unpack, rows),
            out_shape=(
                jax.ShapeDtypeStruct((32, 5, 8, LANES), BF),
                jax.ShapeDtypeStruct((27, 32, 32), F32),
                jax.ShapeDtypeStruct((1, 32), F32),
                jax.ShapeDtypeStruct((27, 32, 32), F32),
                jax.ShapeDtypeStruct((1, 32), F32),
            ),
            in_specs=[vm] * 2,
            out_specs=(hbm,) * 5,
            scratch_shapes=[
                pltpu.VMEM((PAY, LANES), F32),
                pltpu.VMEM((27, 32, 32), F32),
                pltpu.VMEM((27, 32, 32), F32),
                pltpu.VMEM((2, 1, 32), F32),
                dma((13,)),
            ],
            compiler_params=pltpu.CompilerParams(vmem_limit_bytes=16 << 20),
        )(gathered, mid.reshape(5, 32, 8, LANES))
        back = lambda g: g.reshape(3, 3, 3, 32, 32).transpose(3, 0, 1, 2, 4)
        return output[None], back(g1), gb1.reshape(32), back(g2), gb2.reshape(32)

    block = P("smp", None, "gx", None, "gz")
    return jax.shard_map(
        shards, mesh=mesh, in_specs=(block, P(), P(), P(), P(), block),
        out_specs=(block, P(), P(), P(), P()), check_vma=False)
```

```python
import functools

import jax
import jax.numpy as jnp
from jax import lax
from jax.experimental import pallas as pl
from jax.experimental.pallas import tpu as pltpu
from jax.sharding import PartitionSpec as P

MESH = pl.DeviceIdType.MESH
BF = jnp.bfloat16
F32 = jnp.float32
LANES = 128
PAY = 448


def kernel(sizes, scale, feat, cot, w1h, w2h, b1h, b2h, rc, out,
           vf, vc, w1, w2, b1, b2, pm, pe, ps,
           sf, sc, sh, eo, ei, wa, wb, wv, dd, pg, pay, pk, snd, ra, mid, rb, fin,
           ins, hs, hr, as_, ar, bs, br, cs, cr):
    ns, nx, nz = sizes
    hx = min(4, nx)
    nlo = nx // hx
    nzt, ny = nz * nlo, ns // 2
    nr, na = 2 * ny, hx * nzt
    rows = PAY // nr
    smp, gx, gz = lax.axis_index("smp"), lax.axis_index("gx"), lax.axis_index("gz")
    left, right = lax.rem(gx + nx - 1, nx), lax.rem(gx + 1, nx)
    other = 1 - gz
    x_at, z_at = lax.rem(gx, hx), gz * nlo + gx // hx
    y_at, c_at = smp // 2, lax.rem(smp, 2)
    lane = lax.broadcasted_iota(jnp.int32, (32, LANES), 1)
    level = lax.rem(lane // 2, 8)

    def device(x, y, z, c):
        return (y * 2 + c, lax.rem(z, nlo) * hx + x, z // nlo)

    def far(n, m):
        return [(i, j) for i in range(n) for j in range(m) if i or j]

    me_r, me_a = y_at * 2 + c_at, x_at * nzt + z_at
    peers_r, peers_a = [], []
    for i, j in sorted(far(ny, 2), key=lambda o: -2 * min(o[0], ny - o[0]) - o[1]):
        u, c = lax.rem(y_at + i, ny), lax.rem(c_at + j, 2)
        peers_r.append((u * 2 + c, device(x_at, u, z_at, c)))
    for i, j in sorted(far(hx, nzt), key=lambda o: -min(o[0], hx - o[0]) - min(o[1], nzt - o[1])):
        u, v = lax.rem(x_at + i, hx), lax.rem(z_at + j, nzt)
        peers_a.append((u * nzt + v, device(u, y_at, v, c_at)))
    near = ((smp, gx, other), (smp, left, other), (smp, right, other), (smp, left, gz), (smp, right, gz))

    load_f = [pltpu.make_async_copy(feat.at[:, x], vf.at[x], ins.at[x]) for x in range(5)]
    load_c = [pltpu.make_async_copy(cot.at[:, x], vc.at[x], ins.at[5 + x]) for x in range(5)]
    load_w = [
        pltpu.make_async_copy(src, dst, ins.at[10 + i])
        for i, (src, dst) in enumerate(((w1h, w1), (w2h, w2), (b1h, b1), (b2h, b2)))
    ]
    for m in load_f + load_c + load_w:
        m.start()

    barrier = pltpu.get_barrier_semaphore()
    known = [dev for _, dev in peers_r] + [dev for _, dev in peers_a]
    for dev in known:
        pl.semaphore_signal(barrier, inc=1, device_id=dev, device_id_type=MESH)

    def grid(height, width):
        return (lax.broadcasted_iota(jnp.int32, (height, width), 0),
                lax.broadcasted_iota(jnp.int32, (height, width), 1))

    def hot(cond):
        return jnp.where(cond, 1.0, 0.0).astype(BF)

    def first_constants():
        r, c = grid(256, 256)
        pm[...] = hot((r // 32 == lax.rem(c, 8)) & (lax.rem(r, 32) == c // 8))
        r, c = grid(LANES, LANES)
        side = lax.rem(c, 2)
        for x in range(5):
            pe[x * LANES:(x + 1) * LANES] = hot(
                (c // 16 == x) & (((r == LANES - 1) & (side == 0)) | ((r == 0) & (side == 1))))

    def later_constants():
        r, c = grid(LANES, 256)
        beside = hot(((c < LANES) & (c == r + 1)) | ((c >= LANES) & (c == r + LANES - 1)))
        r2 = lax.rem(r, 2)
        ends = ((r2 == 0) & (c == 0)) | ((r2 == 1) & (c == 255))
        for x in range(5):
            ps[x, 0:LANES] = beside
            ps[x, LANES:256] = hot((r // 16 == x) & ends)

    def rows_in(s, v):
        slab = jnp.concatenate([v[x].reshape(256, LANES) for x in range(5)], axis=1)
        moved = jnp.dot(pm[...], slab, preferred_element_type=F32).astype(BF)
        for x in range(5):
            s[1, 1 + x] = moved[:, x * LANES:(x + 1) * LANES]

    def edges(s, f):
        slab = jnp.concatenate([s[1, 1 + x] for x in range(5)], axis=1)
        picked = jnp.dot(slab, pe[...], preferred_element_type=F32)
        acc = jnp.zeros((32, LANES), F32)
        for y in range(8):
            acc = jnp.where(level == y, picked[y * 32:(y + 1) * 32], acc)
        eo[f] = jnp.where(lane < 80, acc, 0.0).astype(BF)

    def halo(s, f):
        plan = (
            (2, eo.at[f], ei.at[f, 1], near[0]),
            (3, eo.at[f], ei.at[f, 2], near[1]),
            (4, eo.at[f], ei.at[f, 0], near[2]),
            (0, s.at[1, 1], s.at[1, 6], near[3]),
            (1, s.at[1, 5], s.at[1, 0], near[4]),
        )
        return [
            pltpu.make_async_remote_copy(
                src_ref=src, dst_ref=dst, send_sem=hs.at[f, i], recv_sem=hr.at[f, i],
                device_id=dev, device_id_type=MESH,
            )
            for i, src, dst, dev in plan
        ]

    def shift(s, f, slots):
        spread = {}
        for slot in slots:
            which, x = (0, 4) if slot == 0 else (2, 0) if slot == 6 else (1, slot - 1)
            if which not in spread:
                e = ei[f, which].astype(F32)
                spread[which] = jnp.concatenate(
                    [jnp.where(level == y, e, 0.0) for y in range(8)], axis=0).astype(BF)
            wide = jnp.concatenate([s[1, slot], spread[which]], axis=1)
            moved = jnp.dot(wide, ps[x], preferred_element_type=F32).astype(BF)
            s[0, slot] = moved[:, :LANES]
            s[2, slot] = moved[:, LANES:]

    def banded(dst, tap):
        zero = jnp.zeros((32, LANES), F32)
        for k in range(9):
            a, c = k // 3, k % 3
            base = jnp.concatenate(tap(a, c) + [jnp.zeros((32, 32), F32)], axis=1)
            r = [pltpu.roll(base, (32 * (m + 3)) % LANES, 1) if m != 1 else base for m in range(4)]
            low, mid_, top = lane < 32, lane < 64, lane >= 96
            tiles = (
                (jnp.where(mid_, r[0], 0.0), zero),
                (r[1], zero),
                (r[2], zero),
                (jnp.where(mid_, 0.0, r[3]), jnp.where(low, r[3], 0.0)),
                (jnp.where(top, r[0], 0.0), jnp.where(mid_, r[0], 0.0)),
                (zero, r[1]),
                (zero, r[2]),
                (zero, jnp.where(mid_, 0.0, r[3])),
            )
            for y, pair in enumerate(tiles):
                for t in range(2):
                    dst[k, y * 32:(y + 1) * 32, t * LANES:(t + 1) * LANES] = pair[t].astype(BF)

    def conv(w, s, xs):
        lhs = jnp.concatenate([w[k] for k in range(9)], axis=1)
        rhs = jnp.concatenate(
            [jnp.concatenate([s[k % 3, x + k // 3] for x in xs], axis=1) for k in range(9)], axis=0)
        return jnp.dot(lhs, rhs, preferred_element_type=F32)

    def diagonal(g):
        t = [[g[y * 32:(y + 1) * 32, u * LANES:(u + 1) * LANES] for u in range(2)] for y in range(8)]
        x0 = jnp.where(lane < 64, t[0][0] + t[4][1], jnp.where(lane >= 96, t[4][0], 0.0))
        x1 = t[1][0] + t[5][1]
        x2 = t[2][0] + t[6][1]
        x3 = jnp.where(lane >= 64, t[3][0] + t[7][1], jnp.where(lane < 32, t[3][1], 0.0))
        total = pltpu.roll(x0, 32, 1) + x1 + pltpu.roll(x2, 96, 1) + pltpu.roll(x3, 64, 1)
        return jnp.where(lane < 96, total, 0.0)

    def column(ref):
        row = lax.broadcasted_iota(jnp.int32, (32, 32), 0)
        col = lax.broadcasted_iota(jnp.int32, (32, 32), 1)
        one = jnp.sum(jnp.where(row == col, jnp.broadcast_to(ref[...], (32, 32)), 0.0), axis=1, keepdims=True)
        return jnp.concatenate([one] * 8, axis=0)

    def taps(w):
        return lambda a, c: [w[a * 9 + b * 3 + c].astype(F32) for b in range(3)]

    def turned(w):
        def tap(a, c):
            wide = jnp.concatenate([w[(2 - a) * 9 + (2 - b) * 3 + 2 - c].astype(F32) for b in range(3)]
                                   + [jnp.zeros((32, 32), F32)], axis=1)
            tall = wide.T
            return [tall[b * 32:(b + 1) * 32] for b in range(3)]
        return tap

    first_constants()
    for m in load_f:
        m.wait()
    rows_in(sf, vf)
    edges(sf, 0)
    for m in load_c:
        m.wait()
    rows_in(sc, vc)
    edges(sc, 1)
    pl.semaphore_wait(barrier, len(known))
    moves_f = halo(sf, 0)
    moves_c = halo(sc, 1)
    for m in moves_f[:3] + moves_c[:3] + moves_f[3:] + moves_c[3:]:
        m.start()
    later_constants()
    for m in load_w:
        m.wait()

    banded(wa, taps(w1))
    banded(wv, turned(w2))

    def folded(v):
        total = v[0:32]
        for y in range(1, 8):
            total = total + v[y * 32:(y + 1) * 32]
        return jnp.sum(total, axis=1, keepdims=True)

    csum = jnp.zeros((256, LANES), F32)
    for x in range(5):
        csum = csum + sc[1, 1 + x].astype(F32)
    csum = folded(csum)

    def split(v, which):
        both = v + pltpu.roll(v, LANES - 2, 1)
        high = both.astype(BF).astype(F32)
        lanes = lax.broadcasted_iota(jnp.int32, v.shape, 1)
        pair = jnp.where(lanes < 98, high, pltpu.roll(both - high, 2, 1))
        return jnp.where(which & (lanes >= 96) & (lanes < 100), pair, v).astype(BF)

    bias = column(b1)
    inner, outer = (1, 2, 3, 4, 5), (0, 6)
    tiles = ((1, 2), (3, 4), (0,))

    def forward(xs):
        v = conv(wa, sf, xs) + bias
        q = 1.0 / (1.0 + jnp.exp(-v))
        h = (v * q).astype(BF)
        d = q * (1.0 + v * (1.0 - q))
        for i, x in enumerate(xs):
            sh[1, 1 + x] = h[:, i * LANES:(i + 1) * LANES]
            dd[x] = d[:, i * LANES:(i + 1) * LANES]

    def backward(xs):
        u = conv(wv, sc, xs)
        part = jnp.zeros((256, LANES), F32)
        for i, x in enumerate(xs):
            p = (u[:, i * LANES:(i + 1) * LANES] * dd[x]).astype(BF)
            pg[x] = p
            part = part + p.astype(F32)
        return part

    for m in moves_f:
        m.wait_recv()
    shift(sf, 0, inner + outer)
    for xs in tiles:
        forward(xs)
    for m in moves_c:
        m.wait_recv()
    shift(sc, 1, inner + outer)
    sums = jnp.zeros((256, LANES), F32)
    for xs in tiles:
        sums = sums + backward(xs)

    found = {}
    def spans(s, c, a):
        return jnp.concatenate([s[c, a + x] for x in range(5)], axis=1)

    def nt(p, r):
        return lax.dot_general(p, r, (((1,), (1,)), ((), ())), preferred_element_type=F32)

    for k in range(9):
        a, c = k // 3, k % 3
        upstream = jnp.concatenate([pg[x] for x in range(5)], axis=1)
        found[k] = diagonal(nt(upstream, spans(sf, c, a)))
    for k in range(9):
        a, c = k // 3, k % 3
        own = jnp.concatenate([sh[1, 1 + x] for x in range(5)], axis=1)
        found[9 + k] = diagonal(nt(spans(sc, 2 - c, 2 - a), own))

    biases = jnp.where(lane == 96, folded(sums), jnp.where(lane == 97, csum, 0.0))
    for n in range(14):
        g, j = n // 3, n % 3
        if n < 12:
            extra = pltpu.roll(found[4 * g + 3], 96 - 32 * j, 1)
            part = jnp.where(lane < 96, found[4 * g + j], extra)
        else:
            part = found[n + 4]
            if n == 13:
                part = part + biases
        pk[n * 32:(n + 1) * 32] = part

    def bias_rows(first):
        r = lax.broadcasted_iota(jnp.int32, (rows, LANES), 0) + first
        return r >= PAY - 32

    for s in range(nr):
        part = pk[s * rows:(s + 1) * rows]
        snd[s] = split(part, bias_rows(s * rows)) if (s + 1) * rows > PAY - 32 else part.astype(BF)

    def remote(src, dst, send, recv, dev):
        return pltpu.make_async_remote_copy(
            src_ref=src, dst_ref=dst, send_sem=send, recv_sem=recv, device_id=dev, device_id_type=MESH)

    out_a = [remote(snd.at[p], ra.at[me_r], as_.at[p], ar.at[me_r], dev) for p, dev in peers_r]
    in_a = [remote(snd.at[p], ra.at[p], as_.at[p], ar.at[p], dev) for p, dev in peers_r]
    out_b = [remote(mid, rb.at[me_a], bs.at[p], br.at[me_a], dev) for p, dev in peers_a]
    in_b = [remote(mid, rb.at[p], bs.at[p], br.at[p], dev) for p, dev in peers_a]
    out_c = [remote(fin, rc.at[me_r], cs.at[p], cr.at[me_r], dev) for p, dev in peers_r]
    in_c = [remote(fin, rc.at[p], cs.at[p], cr.at[p], dev) for p, dev in peers_r]

    for m in out_a:
        m.start()
    ra[me_r] = snd[me_r]
    edges(sh, 2)
    moves_h = halo(sh, 2)
    for m in moves_h:
        m.start()

    def total(ref, n):
        acc = ref[0].astype(F32)
        for s in range(1, n):
            acc = acc + ref[s].astype(F32)
        return acc

    banded(wb, taps(w2))
    bias2 = column(b2)

    def finish(xs):
        v = conv(wb, sh, xs) + bias2
        for i, x in enumerate(xs):
            r = (v[:, i * LANES:(i + 1) * LANES] + sf[1, 1 + x].astype(F32)).astype(BF)
            back = lax.dot_general(pm[...], r, (((0,), (0,)), ((), ())), preferred_element_type=F32)
            out[x] = back.astype(BF)

    for m in in_a:
        m.wait_recv()
    mine = bias_rows(me_r * rows)
    mid[...] = split(total(ra, nr), mine)
    for m in out_b:
        m.start()
    rb[me_a] = mid[...]
    for m in moves_h:
        m.wait_recv()
    shift(sh, 2, inner + outer)
    for xs in tiles:
        finish(xs)
    for m in in_b:
        m.wait_recv()
    fin[...] = split(total(rb, na) * scale, mine)
    for m in out_c:
        m.start()
    rc[me_r] = fin[...]
    for m in moves_f + moves_c + moves_h + out_a + out_b:
        m.wait_send()
    for m in in_c:
        m.wait_recv()
    for m in out_c:
        m.wait_send()

def unpack(rows, rc, mid, out, g1, gb1, g2, gb2, pay, v1, v2, vb, sem):
    moves = [pltpu.make_async_copy(mid.at[x], out.at[:, x], sem.at[x]) for x in range(5)]
    for m in moves:
        m.start()
    for s in range(PAY // rows):
        pay[s * rows:(s + 1) * rows] = rc[s].astype(F32)
    tail = pay[PAY - 32:]
    tail = tail + pltpu.roll(tail, LANES - 2, 1)
    row = lax.broadcasted_iota(jnp.int32, (32, 32), 0)
    col = lax.broadcasted_iota(jnp.int32, (32, 32), 1)

    def send(src, dst):
        moves.append(pltpu.make_async_copy(src, dst, sem.at[len(moves)]))
        moves[-1].start()

    for i, ref in enumerate((gb1, gb2)):
        vb[i] = jnp.sum(jnp.where(row == col, tail[:, 96 + i:97 + i], 0.0), axis=0, keepdims=True)
        send(vb.at[i], ref)
    for n in range(18):
        ref, k = (v1, n) if n < 9 else (v2, n - 9)
        a, c = k // 3, k % 3
        for b in range(3):
            if n >= 16:
                block, place = n - 4, b
            elif n % 4 == 3:
                block, place = 3 * (n // 4) + b, 3
            else:
                block, place = 3 * (n // 4) + n % 4, b
            ref[a * 9 + b * 3 + c] = pay[block * 32:(block + 1) * 32, place * 32:(place + 1) * 32]
        if c == 2:
            part = pl.ds(a * 9, 9)
            send(ref.at[part], (g1 if n < 9 else g2).at[part])
    for m in moves:
        m.wait()


def solution(mesh):
    sizes = tuple(mesh.shape[n] for n in ("smp", "gx", "gz"))
    ns, nx, nz = sizes
    nr, na = ns, nx * nz
    rows = PAY // nr

    def shards(features, first_weight, first_bias, second_weight, second_bias, cotangent):
        cells = ns * nx * nz * 5 * 8 * LANES
        w1 = first_weight.transpose(1, 2, 3, 0, 4).reshape(27, 32, 32)
        w2 = second_weight.transpose(1, 2, 3, 0, 4).reshape(27, 32, 32)
        vm = pl.BlockSpec(memory_space=pltpu.VMEM)
        hbm = pl.BlockSpec(memory_space=pltpu.MemorySpace.HBM)
        dma = pltpu.SemaphoreType.DMA
        gathered, mid = pl.pallas_call(
            functools.partial(kernel, sizes, cells ** -0.5),
            out_shape=(
                jax.ShapeDtypeStruct((nr, rows, LANES), BF),
                jax.ShapeDtypeStruct((5, 256, LANES), BF),
            ),
            in_specs=[hbm] * 6,
            out_specs=(vm,) * 2,
            scratch_shapes=[
                pltpu.VMEM((5, 32, 8, LANES), BF),
                pltpu.VMEM((5, 32, 8, LANES), BF),
                pltpu.VMEM((27, 32, 32), BF),
                pltpu.VMEM((27, 32, 32), BF),
                pltpu.VMEM((1, 32), F32),
                pltpu.VMEM((1, 32), F32),
                pltpu.VMEM((256, 256), BF),
                pltpu.VMEM((640, LANES), BF),
                pltpu.VMEM((5, 256, 256), BF),
                pltpu.VMEM((3, 7, 256, LANES), BF),
                pltpu.VMEM((3, 7, 256, LANES), BF),
                pltpu.VMEM((3, 7, 256, LANES), BF),
                pltpu.VMEM((3, 32, LANES), BF),
                pltpu.VMEM((3, 3, 32, LANES), BF),
                pltpu.VMEM((9, 256, 256), BF),
                pltpu.VMEM((9, 256, 256), BF),
                pltpu.VMEM((9, 256, 256), BF),
                pltpu.VMEM((5, 256, LANES), F32),
                pltpu.VMEM((5, 256, LANES), BF),
                pltpu.VMEM((576, LANES), F32),
                pltpu.VMEM((PAY, LANES), F32),
                pltpu.VMEM((nr, rows, LANES), BF),
                pltpu.VMEM((nr, rows, LANES), BF),
                pltpu.VMEM((rows, LANES), BF),
                pltpu.VMEM((na, rows, LANES), BF),
                pltpu.VMEM((rows, LANES), BF),
                dma((14,)), dma((3, 5)), dma((3, 5)),
                dma((nr,)), dma((nr,)), dma((na,)), dma((na,)), dma((nr,)), dma((nr,)),
            ],
            compiler_params=pltpu.CompilerParams(
                collective_id=0, has_side_effects=True, vmem_limit_bytes=32 << 20),
        )(*(pltpu.with_memory_space_constraint(v, pltpu.MemorySpace.HBM) for v in (
            features[0], cotangent[0], w1, w2, first_bias.reshape(1, 32), second_bias.reshape(1, 32))))
        output, g1, gb1, g2, gb2 = pl.pallas_call(
            functools.partial(unpack, rows),
            out_shape=(
                jax.ShapeDtypeStruct((32, 5, 8, LANES), BF),
                jax.ShapeDtypeStruct((27, 32, 32), F32),
                jax.ShapeDtypeStruct((1, 32), F32),
                jax.ShapeDtypeStruct((27, 32, 32), F32),
                jax.ShapeDtypeStruct((1, 32), F32),
            ),
            in_specs=[vm] * 2,
            out_specs=(hbm,) * 5,
            scratch_shapes=[
                pltpu.VMEM((PAY, LANES), F32),
                pltpu.VMEM((27, 32, 32), F32),
                pltpu.VMEM((27, 32, 32), F32),
                pltpu.VMEM((2, 1, 32), F32),
                dma((13,)),
            ],
            compiler_params=pltpu.CompilerParams(vmem_limit_bytes=16 << 20),
        )(gathered, mid.reshape(5, 32, 8, LANES))
        back = lambda g: g.reshape(3, 3, 3, 32, 32).transpose(3, 0, 1, 2, 4)
        return output[None], back(g1), gb1.reshape(32), back(g2), gb2.reshape(32)

    block = P("smp", None, "gx", None, "gz")
    return jax.shard_map(
        shards, mesh=mesh, in_specs=(block, P(), P(), P(), P(), block),
        out_specs=(block, P(), P(), P(), P()), check_vma=False)
```

```python
import functools

import jax
import jax.numpy as jnp
from jax import lax
from jax.experimental import pallas as pl
from jax.experimental.pallas import tpu as pltpu
from jax.sharding import PartitionSpec as P

MESH = pl.DeviceIdType.MESH
BF = jnp.bfloat16
F32 = jnp.float32
LANES = 128
PAY = 448


def kernel(sizes, scale, feat, cot, w1h, w2h, b1h, b2h, rc, out,
           vf, vc, w1, w2, b1, b2, pm, pe, ps,
           sf, sc, sh, eo, ei, wa, wb, wv, dd, pg, pay, pk, snd, ra, mid, rb, fin,
           ins, hs, hr, as_, ar, bs, br, cs, cr):
    ns, nx, nz = sizes
    hx = min(4, nx)
    nlo = nx // hx
    nzt, ny = nz * nlo, ns // 2
    nr, na = 2 * ny, hx * nzt
    rows = PAY // nr
    smp, gx, gz = lax.axis_index("smp"), lax.axis_index("gx"), lax.axis_index("gz")
    left, right = lax.rem(gx + nx - 1, nx), lax.rem(gx + 1, nx)
    other = 1 - gz
    x_at, z_at = lax.rem(gx, hx), gz * nlo + gx // hx
    y_at, c_at = smp // 2, lax.rem(smp, 2)
    lane = lax.broadcasted_iota(jnp.int32, (32, LANES), 1)
    level = lax.rem(lane // 2, 8)

    def device(x, y, z, c):
        return (y * 2 + c, lax.rem(z, nlo) * hx + x, z // nlo)

    def far(n, m):
        return [(i, j) for i in range(n) for j in range(m) if i or j]

    me_r, me_a = y_at * 2 + c_at, x_at * nzt + z_at
    peers_r, peers_a = [], []
    for i, j in sorted(far(ny, 2), key=lambda o: -2 * min(o[0], ny - o[0]) - o[1]):
        u, c = lax.rem(y_at + i, ny), lax.rem(c_at + j, 2)
        peers_r.append((u * 2 + c, device(x_at, u, z_at, c)))
    for i, j in sorted(far(hx, nzt), key=lambda o: -min(o[0], hx - o[0]) - min(o[1], nzt - o[1])):
        u, v = lax.rem(x_at + i, hx), lax.rem(z_at + j, nzt)
        peers_a.append((u * nzt + v, device(u, y_at, v, c_at)))
    near = ((smp, gx, other), (smp, left, other), (smp, right, other), (smp, left, gz), (smp, right, gz))

    load_f = [pltpu.make_async_copy(feat.at[:, x], vf.at[x], ins.at[x]) for x in range(5)]
    load_c = [pltpu.make_async_copy(cot.at[:, x], vc.at[x], ins.at[5 + x]) for x in range(5)]
    load_w = [
        pltpu.make_async_copy(src, dst, ins.at[10 + i])
        for i, (src, dst) in enumerate(((w1h, w1), (w2h, w2), (b1h, b1), (b2h, b2)))
    ]
    for m in load_f + load_c + load_w:
        m.start()

    barrier = pltpu.get_barrier_semaphore()
    known = [dev for _, dev in peers_r] + [dev for _, dev in peers_a]
    for dev in known:
        pl.semaphore_signal(barrier, inc=1, device_id=dev, device_id_type=MESH)

    def grid(height, width):
        return (lax.broadcasted_iota(jnp.int32, (height, width), 0),
                lax.broadcasted_iota(jnp.int32, (height, width), 1))

    def hot(cond):
        return jnp.where(cond, 1.0, 0.0).astype(BF)

    def first_constants():
        r, c = grid(256, 256)
        pm[...] = hot((r // 32 == lax.rem(c, 8)) & (lax.rem(r, 32) == c // 8))
        r, c = grid(LANES, LANES)
        side = lax.rem(c, 2)
        for x in range(5):
            pe[x * LANES:(x + 1) * LANES] = hot(
                (c // 16 == x) & (((r == LANES - 1) & (side == 0)) | ((r == 0) & (side == 1))))

    def later_constants():
        r, c = grid(LANES, 256)
        beside = hot(((c < LANES) & (c == r + 1)) | ((c >= LANES) & (c == r + LANES - 1)))
        r2 = lax.rem(r, 2)
        ends = ((r2 == 0) & (c == 0)) | ((r2 == 1) & (c == 255))
        for x in range(5):
            ps[x, 0:LANES] = beside
            ps[x, LANES:256] = hot((r // 16 == x) & ends)

    def rows_in(s, v):
        slab = jnp.concatenate([v[x].reshape(256, LANES) for x in range(5)], axis=1)
        moved = jnp.dot(pm[...], slab, preferred_element_type=F32).astype(BF)
        for x in range(5):
            s[1, 1 + x] = moved[:, x * LANES:(x + 1) * LANES]

    def edges(s, f):
        slab = jnp.concatenate([s[1, 1 + x] for x in range(5)], axis=1)
        picked = jnp.dot(slab, pe[...], preferred_element_type=F32)
        acc = jnp.zeros((32, LANES), F32)
        for y in range(8):
            acc = jnp.where(level == y, picked[y * 32:(y + 1) * 32], acc)
        eo[f] = jnp.where(lane < 80, acc, 0.0).astype(BF)

    def halo(s, f):
        plan = (
            (2, eo.at[f], ei.at[f, 1], near[0]),
            (3, eo.at[f], ei.at[f, 2], near[1]),
            (4, eo.at[f], ei.at[f, 0], near[2]),
            (0, s.at[1, 1], s.at[1, 6], near[3]),
            (1, s.at[1, 5], s.at[1, 0], near[4]),
        )
        return [
            pltpu.make_async_remote_copy(
                src_ref=src, dst_ref=dst, send_sem=hs.at[f, i], recv_sem=hr.at[f, i],
                device_id=dev, device_id_type=MESH,
            )
            for i, src, dst, dev in plan
        ]

    def shift(s, f, slots):
        spread = {}
        for slot in slots:
            which, x = (0, 4) if slot == 0 else (2, 0) if slot == 6 else (1, slot - 1)
            if which not in spread:
                e = ei[f, which].astype(F32)
                spread[which] = jnp.concatenate(
                    [jnp.where(level == y, e, 0.0) for y in range(8)], axis=0).astype(BF)
            wide = jnp.concatenate([s[1, slot], spread[which]], axis=1)
            moved = jnp.dot(wide, ps[x], preferred_element_type=F32).astype(BF)
            s[0, slot] = moved[:, :LANES]
            s[2, slot] = moved[:, LANES:]

    def banded(dst, tap):
        zero = jnp.zeros((32, LANES), F32)
        for k in range(9):
            a, c = k // 3, k % 3
            base = jnp.concatenate(tap(a, c) + [jnp.zeros((32, 32), F32)], axis=1)
            r = [pltpu.roll(base, (32 * (m + 3)) % LANES, 1) if m != 1 else base for m in range(4)]
            low, mid_, top = lane < 32, lane < 64, lane >= 96
            tiles = (
                (jnp.where(mid_, r[0], 0.0), zero),
                (r[1], zero),
                (r[2], zero),
                (jnp.where(mid_, 0.0, r[3]), jnp.where(low, r[3], 0.0)),
                (jnp.where(top, r[0], 0.0), jnp.where(mid_, r[0], 0.0)),
                (zero, r[1]),
                (zero, r[2]),
                (zero, jnp.where(mid_, 0.0, r[3])),
            )
            for y, pair in enumerate(tiles):
                for t in range(2):
                    dst[k, y * 32:(y + 1) * 32, t * LANES:(t + 1) * LANES] = pair[t].astype(BF)

    def conv(w, s, xs):
        lhs = jnp.concatenate([w[k] for k in range(9)], axis=1)
        rhs = jnp.concatenate(
            [jnp.concatenate([s[k % 3, x + k // 3] for x in xs], axis=1) for k in range(9)], axis=0)
        return jnp.dot(lhs, rhs, preferred_element_type=F32)

    def diagonal(g):
        t = [[g[y * 32:(y + 1) * 32, u * LANES:(u + 1) * LANES] for u in range(2)] for y in range(8)]
        x0 = jnp.where(lane < 64, t[0][0] + t[4][1], jnp.where(lane >= 96, t[4][0], 0.0))
        x1 = t[1][0] + t[5][1]
        x2 = t[2][0] + t[6][1]
        x3 = jnp.where(lane >= 64, t[3][0] + t[7][1], jnp.where(lane < 32, t[3][1], 0.0))
        total = pltpu.roll(x0, 32, 1) + x1 + pltpu.roll(x2, 96, 1) + pltpu.roll(x3, 64, 1)
        return jnp.where(lane < 96, total, 0.0)

    def column(ref):
        row = lax.broadcasted_iota(jnp.int32, (32, 32), 0)
        col = lax.broadcasted_iota(jnp.int32, (32, 32), 1)
        one = jnp.sum(jnp.where(row == col, jnp.broadcast_to(ref[...], (32, 32)), 0.0), axis=1, keepdims=True)
        return jnp.concatenate([one] * 8, axis=0)

    def taps(w):
        return lambda a, c: [w[a * 9 + b * 3 + c].astype(F32) for b in range(3)]

    def turned(w):
        def tap(a, c):
            wide = jnp.concatenate([w[(2 - a) * 9 + (2 - b) * 3 + 2 - c].astype(F32) for b in range(3)]
                                   + [jnp.zeros((32, 32), F32)], axis=1)
            tall = wide.T
            return [tall[b * 32:(b + 1) * 32] for b in range(3)]
        return tap

    first_constants()
    for m in load_f:
        m.wait()
    rows_in(sf, vf)
    edges(sf, 0)
    for m in load_c:
        m.wait()
    rows_in(sc, vc)
    edges(sc, 1)
    pl.semaphore_wait(barrier, len(known))
    moves_f = halo(sf, 0)
    moves_c = halo(sc, 1)
    for m in moves_f[:3] + moves_c[:3] + moves_f[3:] + moves_c[3:]:
        m.start()
    later_constants()
    for m in load_w:
        m.wait()

    banded(wa, taps(w1))
    banded(wv, turned(w2))

    def folded(v):
        total = v[0:32]
        for y in range(1, 8):
            total = total + v[y * 32:(y + 1) * 32]
        return jnp.sum(total, axis=1, keepdims=True)

    csum = jnp.zeros((256, LANES), F32)
    for x in range(5):
        csum = csum + sc[1, 1 + x].astype(F32)
    csum = folded(csum)

    def split(v, which):
        both = v + pltpu.roll(v, LANES - 2, 1)
        high = both.astype(BF).astype(F32)
        lanes = lax.broadcasted_iota(jnp.int32, v.shape, 1)
        pair = jnp.where(lanes < 98, high, pltpu.roll(both - high, 2, 1))
        return jnp.where(which & (lanes >= 96) & (lanes < 100), pair, v).astype(BF)

    bias = column(b1)
    inner, outer = (1, 2, 3, 4, 5), (0, 6)
    tiles = ((1, 2), (3, 4), (0,))

    def forward(xs):
        v = conv(wa, sf, xs) + bias
        q = 1.0 / (1.0 + jnp.exp(-v))
        h = (v * q).astype(BF)
        d = q * (1.0 + v * (1.0 - q))
        for i, x in enumerate(xs):
            sh[1, 1 + x] = h[:, i * LANES:(i + 1) * LANES]
            dd[x] = d[:, i * LANES:(i + 1) * LANES]

    def backward(xs):
        u = conv(wv, sc, xs)
        part = jnp.zeros((256, LANES), F32)
        for i, x in enumerate(xs):
            p = (u[:, i * LANES:(i + 1) * LANES] * dd[x]).astype(BF)
            pg[x] = p
            part = part + p.astype(F32)
        return part

    for m in moves_f:
        m.wait_recv()
    shift(sf, 0, inner + outer)
    for xs in tiles:
        forward(xs)
    for m in moves_c:
        m.wait_recv()
    shift(sc, 1, inner + outer)
    found = {}
    def spans(s, c, a):
        return jnp.concatenate([s[c, a + x] for x in range(5)], axis=1)

    def nt(p, r):
        return lax.dot_general(p, r, (((1,), (1,)), ((), ())), preferred_element_type=F32)

    for k in range(9):
        a, c = k // 3, k % 3
        own = jnp.concatenate([sh[1, 1 + x] for x in range(5)], axis=1)
        found[9 + k] = diagonal(nt(spans(sc, 2 - c, 2 - a), own))

    sums = jnp.zeros((256, LANES), F32)
    for xs in tiles:
        sums = sums + backward(xs)

    for k in range(9):
        a, c = k // 3, k % 3
        upstream = jnp.concatenate([pg[x] for x in range(5)], axis=1)
        found[k] = diagonal(nt(upstream, spans(sf, c, a)))
    biases = jnp.where(lane == 96, folded(sums), jnp.where(lane == 97, csum, 0.0))
    for n in range(14):
        g, j = n // 3, n % 3
        if n < 12:
            extra = pltpu.roll(found[4 * g + 3], 96 - 32 * j, 1)
            part = jnp.where(lane < 96, found[4 * g + j], extra)
        else:
            part = found[n + 4]
            if n == 13:
                part = part + biases
        pk[n * 32:(n + 1) * 32] = part

    def bias_rows(first):
        r = lax.broadcasted_iota(jnp.int32, (rows, LANES), 0) + first
        return r >= PAY - 32

    for s in range(nr):
        part = pk[s * rows:(s + 1) * rows]
        snd[s] = split(part, bias_rows(s * rows)) if (s + 1) * rows > PAY - 32 else part.astype(BF)

    def remote(src, dst, send, recv, dev):
        return pltpu.make_async_remote_copy(
            src_ref=src, dst_ref=dst, send_sem=send, recv_sem=recv, device_id=dev, device_id_type=MESH)

    out_a = [remote(snd.at[p], ra.at[me_r], as_.at[p], ar.at[me_r], dev) for p, dev in peers_r]
    in_a = [remote(snd.at[p], ra.at[p], as_.at[p], ar.at[p], dev) for p, dev in peers_r]
    out_b = [remote(mid, rb.at[me_a], bs.at[p], br.at[me_a], dev) for p, dev in peers_a]
    in_b = [remote(mid, rb.at[p], bs.at[p], br.at[p], dev) for p, dev in peers_a]
    out_c = [remote(fin, rc.at[me_r], cs.at[p], cr.at[me_r], dev) for p, dev in peers_r]
    in_c = [remote(fin, rc.at[p], cs.at[p], cr.at[p], dev) for p, dev in peers_r]

    for m in out_a:
        m.start()
    ra[me_r] = snd[me_r]
    edges(sh, 2)
    moves_h = halo(sh, 2)
    for m in moves_h:
        m.start()

    def total(ref, n):
        acc = ref[0].astype(F32)
        for s in range(1, n):
            acc = acc + ref[s].astype(F32)
        return acc

    banded(wb, taps(w2))
    bias2 = column(b2)

    def finish(xs):
        v = conv(wb, sh, xs) + bias2
        for i, x in enumerate(xs):
            r = (v[:, i * LANES:(i + 1) * LANES] + sf[1, 1 + x].astype(F32)).astype(BF)
            back = lax.dot_general(pm[...], r, (((0,), (0,)), ((), ())), preferred_element_type=F32)
            out[x] = back.astype(BF)

    for m in in_a:
        m.wait_recv()
    mine = bias_rows(me_r * rows)
    mid[...] = split(total(ra, nr), mine)
    for m in out_b:
        m.start()
    rb[me_a] = mid[...]
    for m in moves_h:
        m.wait_recv()
    shift(sh, 2, inner + outer)
    for xs in tiles:
        finish(xs)
    for m in in_b:
        m.wait_recv()
    fin[...] = split(total(rb, na) * scale, mine)
    for m in out_c:
        m.start()
    rc[me_r] = fin[...]
    for m in moves_f + moves_c + moves_h + out_a + out_b:
        m.wait_send()
    for m in in_c:
        m.wait_recv()
    for m in out_c:
        m.wait_send()

def unpack(rows, rc, mid, out, g1, gb1, g2, gb2, pay, v1, v2, vb, sem):
    moves = [pltpu.make_async_copy(mid.at[x], out.at[:, x], sem.at[x]) for x in range(5)]
    for m in moves:
        m.start()
    for s in range(PAY // rows):
        pay[s * rows:(s + 1) * rows] = rc[s].astype(F32)
    tail = pay[PAY - 32:]
    tail = tail + pltpu.roll(tail, LANES - 2, 1)
    row = lax.broadcasted_iota(jnp.int32, (32, 32), 0)
    col = lax.broadcasted_iota(jnp.int32, (32, 32), 1)

    def send(src, dst):
        moves.append(pltpu.make_async_copy(src, dst, sem.at[len(moves)]))
        moves[-1].start()

    for i, ref in enumerate((gb1, gb2)):
        vb[i] = jnp.sum(jnp.where(row == col, tail[:, 96 + i:97 + i], 0.0), axis=0, keepdims=True)
        send(vb.at[i], ref)
    for n in range(18):
        ref, k = (v1, n) if n < 9 else (v2, n - 9)
        a, c = k // 3, k % 3
        for b in range(3):
            if n >= 16:
                block, place = n - 4, b
            elif n % 4 == 3:
                block, place = 3 * (n // 4) + b, 3
            else:
                block, place = 3 * (n // 4) + n % 4, b
            ref[a * 9 + b * 3 + c] = pay[block * 32:(block + 1) * 32, place * 32:(place + 1) * 32]
        if c == 2:
            part = pl.ds(a * 9, 9)
            send(ref.at[part], (g1 if n < 9 else g2).at[part])
    for m in moves:
        m.wait()


def solution(mesh):
    sizes = tuple(mesh.shape[n] for n in ("smp", "gx", "gz"))
    ns, nx, nz = sizes
    nr, na = ns, nx * nz
    rows = PAY // nr

    def shards(features, first_weight, first_bias, second_weight, second_bias, cotangent):
        cells = ns * nx * nz * 5 * 8 * LANES
        w1 = first_weight.transpose(1, 2, 3, 0, 4).reshape(27, 32, 32)
        w2 = second_weight.transpose(1, 2, 3, 0, 4).reshape(27, 32, 32)
        vm = pl.BlockSpec(memory_space=pltpu.VMEM)
        hbm = pl.BlockSpec(memory_space=pltpu.MemorySpace.HBM)
        dma = pltpu.SemaphoreType.DMA
        gathered, mid = pl.pallas_call(
            functools.partial(kernel, sizes, cells ** -0.5),
            out_shape=(
                jax.ShapeDtypeStruct((nr, rows, LANES), BF),
                jax.ShapeDtypeStruct((5, 256, LANES), BF),
            ),
            in_specs=[hbm] * 6,
            out_specs=(vm,) * 2,
            scratch_shapes=[
                pltpu.VMEM((5, 32, 8, LANES), BF),
                pltpu.VMEM((5, 32, 8, LANES), BF),
                pltpu.VMEM((27, 32, 32), BF),
                pltpu.VMEM((27, 32, 32), BF),
                pltpu.VMEM((1, 32), F32),
                pltpu.VMEM((1, 32), F32),
                pltpu.VMEM((256, 256), BF),
                pltpu.VMEM((640, LANES), BF),
                pltpu.VMEM((5, 256, 256), BF),
                pltpu.VMEM((3, 7, 256, LANES), BF),
                pltpu.VMEM((3, 7, 256, LANES), BF),
                pltpu.VMEM((3, 7, 256, LANES), BF),
                pltpu.VMEM((3, 32, LANES), BF),
                pltpu.VMEM((3, 3, 32, LANES), BF),
                pltpu.VMEM((9, 256, 256), BF),
                pltpu.VMEM((9, 256, 256), BF),
                pltpu.VMEM((9, 256, 256), BF),
                pltpu.VMEM((5, 256, LANES), F32),
                pltpu.VMEM((5, 256, LANES), BF),
                pltpu.VMEM((576, LANES), F32),
                pltpu.VMEM((PAY, LANES), F32),
                pltpu.VMEM((nr, rows, LANES), BF),
                pltpu.VMEM((nr, rows, LANES), BF),
                pltpu.VMEM((rows, LANES), BF),
                pltpu.VMEM((na, rows, LANES), BF),
                pltpu.VMEM((rows, LANES), BF),
                dma((14,)), dma((3, 5)), dma((3, 5)),
                dma((nr,)), dma((nr,)), dma((na,)), dma((na,)), dma((nr,)), dma((nr,)),
            ],
            compiler_params=pltpu.CompilerParams(
                collective_id=0, has_side_effects=True, vmem_limit_bytes=32 << 20),
        )(*(pltpu.with_memory_space_constraint(v, pltpu.MemorySpace.HBM) for v in (
            features[0], cotangent[0], w1, w2, first_bias.reshape(1, 32), second_bias.reshape(1, 32))))
        output, g1, gb1, g2, gb2 = pl.pallas_call(
            functools.partial(unpack, rows),
            out_shape=(
                jax.ShapeDtypeStruct((32, 5, 8, LANES), BF),
                jax.ShapeDtypeStruct((27, 32, 32), F32),
                jax.ShapeDtypeStruct((1, 32), F32),
                jax.ShapeDtypeStruct((27, 32, 32), F32),
                jax.ShapeDtypeStruct((1, 32), F32),
            ),
            in_specs=[vm] * 2,
            out_specs=(hbm,) * 5,
            scratch_shapes=[
                pltpu.VMEM((PAY, LANES), F32),
                pltpu.VMEM((27, 32, 32), F32),
                pltpu.VMEM((27, 32, 32), F32),
                pltpu.VMEM((2, 1, 32), F32),
                dma((13,)),
            ],
            compiler_params=pltpu.CompilerParams(vmem_limit_bytes=16 << 20),
        )(gathered, mid.reshape(5, 32, 8, LANES))
        back = lambda g: g.reshape(3, 3, 3, 32, 32).transpose(3, 0, 1, 2, 4)
        return output[None], back(g1), gb1.reshape(32), back(g2), gb2.reshape(32)

    block = P("smp", None, "gx", None, "gz")
    return jax.shard_map(
        shards, mesh=mesh, in_specs=(block, P(), P(), P(), P(), block),
        out_specs=(block, P(), P(), P(), P()), check_vma=False)
```
